128 devices in a mesh: ctx: 16 (over z, x_lo, core), tp: 8 (over y, x_hi).
Axes of the slice: x: 4 (x_hi: 2, x_lo: 2; x = x_hi * 2 + x_lo), y: 4, z: 4, core: 2. Of those that a mesh axis runs over, the one named last changes fastest.
Arguments:
- projected: bfloat16 [3, 4096, 8192], P(None, 'ctx', 'tp'), may hold values from -6 to 6
- short_taps: float32 [3, 7, 8192], P(None, None, 'tp'), may hold values from -2.4 to 2.4
- range_filter: bfloat16 [64, 1024], P('tp'), may hold values from -0.1875 to 0.1875
- skip_gain: float32 [8192], P('tp'), may hold values from -4 to 4
- out_weight: bfloat16 [8192, 8192], P('ctx', 'tp'), may hold values from -0.0625 to 0.0625
Outputs:
- mixed: bfloat16 [4096, 8192], P('ctx', 'tp')
The draws below stay inside these ranges and needn't reach their ends.
All inputs are finite; a program needn't handle non-finite values.
Results may differ from the reference program's by a relative error of at most 0.0057.
Values may be sent and summed in bfloat16 or wider, within the bound.
A program may use at most 192 MiB of HBM per device.

```python
import jax
import jax.numpy as jnp
from jax import lax

D = 8192
KTAPS = 7
GRP = 128
FILT = 1024
GROUPS = 64
TOKENS = 4096


def block_levels(own_key, extent, shards, low, largest):
    def one(dim, shards_of):
        draws = jax.random.uniform(jax.random.fold_in(jax.random.fold_in(own_key, 6), dim), (shards_of,), jnp.float32, low / len(shards), largest / len(shards))
        return jnp.repeat(jnp.exp(draws), extent[dim] // shards_of).reshape((-1,) + (1,) * (len(extent) - dim - 1))

    level = one(*shards[0])
    for cut in shards[1:]:
        level = level * one(*cut)
    return level


def scatter_about(key, dims, scale, limit, cuts=(), held_as=jnp.bfloat16):
    values = jax.random.normal(key, dims, jnp.float32) * scale
    if len(cuts) > 0:
        values = block_levels(key, dims, cuts, -0.22, 0.18) * values
    return jnp.clip(values, min=-limit, max=limit).astype(held_as)


def setup_inputs(seed: int = 0) -> dict:
    splits = jax.random.split(jax.random.key(seed), 6)
    return {
        "projected": scatter_about(splits[0], (3, TOKENS, D), 1.0, 6.0, ((1, 16), (2, 8))),
        "short_taps": scatter_about(splits[1], (3, KTAPS, D), 0.4, 2.4, ((2, 8),), jnp.float32),
        "range_filter": scatter_about(splits[2], (GROUPS, FILT), FILT ** -0.5, 0.1875, ((0, 8),)),
        "skip_gain": scatter_about(splits[3], (D,), 1.0, 4.0, ((0, 8),), jnp.float32),
        "out_weight": scatter_about(splits[4], (D, D), D ** -0.5, 0.0625, ((0, 16), (1, 8))),
    }


def short_conv(signal, tap_rows):
    accumulated = jnp.zeros(signal.shape, jnp.float32)
    for lag_index in range(KTAPS):
        accumulated = accumulated + tap_rows[lag_index][None, :] * jnp.roll(signal, lag_index, axis=0).astype(jnp.float32)
    return accumulated


def reference(projected, short_taps, range_filter, skip_gain, out_weight):
    query_feat = short_conv(projected[0], short_taps[0])
    key_feat = short_conv(projected[1], short_taps[1])
    value_feat = short_conv(projected[2], short_taps[2])
    mixed_in = (key_feat * value_feat).astype(jnp.bfloat16)
    restored = lax.optimization_barrier(mixed_in).astype(jnp.float32)
    padded_filter = jnp.concatenate([range_filter.astype(jnp.float32).T, jnp.zeros((TOKENS - FILT, GROUPS), jnp.float32)], axis=0)
    spectrum = jnp.fft.rfft(restored, axis=0).reshape(TOKENS // 2 + 1, GROUPS, GRP)
    filter_spectrum = jnp.fft.rfft(padded_filter, axis=0)
    toeplitz = jnp.fft.irfft(spectrum * filter_spectrum[:, :, None], n=TOKENS, axis=0).reshape(TOKENS, D)
    gated_out = (query_feat * (toeplitz + skip_gain[None, :] * restored)).astype(jnp.bfloat16)
    return jnp.dot(gated_out, out_weight, preferred_element_type=jnp.float32).astype(jnp.bfloat16)
```

```python
import jax
import jax.numpy as jnp
from jax import lax
from jax.sharding import PartitionSpec as P


def passed_along(block, axis, distance):
    devices = range(lax.axis_size(axis))
    route = [((i - distance) % len(devices), i) for i in devices]
    return lax.ppermute(block, axis, route)


def short_conv(extended, tap_rows, length):
    accumulated = jnp.zeros((length, extended.shape[1]), jnp.float32)
    rim_width = tap_rows.shape[0] - 1
    for lag_index in range(tap_rows.shape[0]):
        window = extended[rim_width - lag_index : rim_width - lag_index + length]
        accumulated = accumulated + tap_rows[lag_index][None, :] * window.astype(jnp.float32)
    return accumulated


def toeplitz_strip(range_filter, length):
    groups, kept = range_filter.shape
    period = kept + 2 * length
    flipped = range_filter[:, ::-1]
    row = jnp.pad(flipped, ((0, 0), (length, period - length - kept)))
    tiled = jnp.tile(row, (1, length + 1))
    start = length - 1
    shifted = tiled[:, start : start + length * (period - 1)].reshape(groups, length, period - 1)
    return shifted[:, :, : kept + length]


def local(projected, short_taps, range_filter, skip_gain, out_weight):
    length = projected.shape[1]
    width_dev = projected.shape[2]
    groups = range_filter.shape[0]
    group_width = width_dev // groups
    rim_width = short_taps.shape[1] - 1
    span_blocks = range_filter.shape[1] // length
    rim_block = passed_along(projected[:, length - rim_width :, :], "ctx", 1)
    extended = jnp.concatenate([rim_block, projected], axis=1)
    query_feat = short_conv(extended[0], short_taps[0], length)
    key_feat = short_conv(extended[1], short_taps[1], length)
    value_feat = short_conv(extended[2], short_taps[2], length)
    mixed_in = (key_feat * value_feat).astype(jnp.bfloat16)
    strip = toeplitz_strip(range_filter, length)
    pieces = [passed_along(mixed_in, "ctx", offset) for offset in range(span_blocks, 0, -1)]
    window = jnp.concatenate(pieces + [mixed_in], axis=0).reshape(-1, groups, group_width)
    toeplitz = jnp.einsum("gam,mgc->agc", strip, window, preferred_element_type=jnp.float32)
    toeplitz = toeplitz.reshape(length, width_dev)
    restored = lax.optimization_barrier(mixed_in).astype(jnp.float32)
    gated_out = (query_feat * (toeplitz + skip_gain[None, :] * restored)).astype(jnp.bfloat16)
    gathered = lax.all_gather(gated_out, "tp", axis=1, tiled=True)
    summed = jnp.dot(
        gathered,
        lax.all_gather(out_weight, "ctx", axis=0, tiled=True),
        preferred_element_type=jnp.float32,
    )
    return summed.astype(jnp.bfloat16)


def solution(mesh):
    placed = (P(None, "ctx", "tp"), P(None, None, "tp"), P("tp", None), P("tp"), P("ctx", "tp"))
    return jax.shard_map(
        local, mesh=mesh, in_specs=placed, out_specs=P("ctx", "tp"), check_vma=False
    )
```

```python
import functools

import jax
import jax.numpy as jnp
from jax import lax
from jax.experimental import pallas as pl
from jax.experimental.pallas import tpu as pltpu
from jax.sharding import PartitionSpec as P

MESH = pl.DeviceIdType.MESH
RIM = 16
CHUNKS = 4
RING = 4
QUAD = 4
UPWARD = (2,)
ORDER = (3, 2, 1, 0)


def short_conv(extended, tap_rows):
    acc = tap_rows[0] * extended[RIM:]
    for lag in range(1, len(tap_rows)):
        acc = acc + tap_rows[lag] * pltpu.roll(extended, lag, axis=0)[RIM:]
    return acc


def kernel(
    proj, taps, filt, gain, w, out,
    rim, qext, qfeat, mixsend, seq, flipped, strip, abuf, wbuf, csend, crecv,
    rim_s, rim_r, q_s, q_r, qrim_s, qrim_r, mix_s, mix_r, halo_s, halo_r,
    wx_s, wx_r, wz_s, wz_r, w2_s, w2_r, a_s, a_r, a2_s, a2_r, p_s, p_r, c_s, c_r,
):
    length = proj.shape[1]
    piece = proj.shape[2] // QUAD
    ktaps = taps.shape[1]
    groups_here = strip.shape[0]
    group_width = piece // groups_here
    kept = filt.shape[1]
    shard = w.shape[0]
    ncol = w.shape[1] // CHUNKS
    half = length // 2
    rows_step = length // 4
    f32, bf16 = jnp.float32, jnp.bfloat16

    ctx, tp = lax.axis_index("ctx"), lax.axis_index("tp")
    z, r = ctx // QUAD, ctx % QUAD
    lo, c = r // 2, r % 2
    y, hi = tp // 2, tp % 2
    zu, zd = (z + 1) % RING, (z + RING - 1) % RING
    yu, yd = (y + 1) % RING, (y + RING - 1) % RING
    z2, y2 = (z + 2) % RING, (y + 2) % RING

    def flip(s):
        b1 = 1 - lo if s & 2 else lo
        b0 = 1 - c if s & 1 else c
        return 2 * b1 + b0

    def at(ctx_, tp_):
        return {"ctx": ctx_, "tp": tp_}

    up, down = at(zu * QUAD + r, tp), at(zd * QUAD + r, tp)
    right, left = at(ctx, yu * 2 + hi), at(ctx, yd * 2 + hi)
    partner = at(z * QUAD + flip(1), tp)

    def rcopy(src, dst, ssem, rsem, dev):
        return pltpu.make_async_remote_copy(
            src_ref=src, dst_ref=dst, send_sem=ssem, recv_sem=rsem, device_id=dev, device_id_type=MESH
        )

    def landed(dst, rsem):
        pltpu.make_async_copy(dst, dst, rsem).wait()

    sent = []

    def send(src, dst, ssem, rsem, dev):
        copy = rcopy(src, dst, ssem, rsem, dev)
        copy.start()
        sent.append(copy)

    barrier = pltpu.get_barrier_semaphore()
    peers = [at(z * QUAD + flip(s), tp) for s in range(1, QUAD)]
    peers += [at(z * QUAD + s, y * 2 + 1 - hi) for s in range(QUAD)]
    peers += [at(zz * QUAD + s, tp) for zz in (zu, zd) for s in range(QUAD)]
    peers += [right, left]
    for dev in peers:
        pl.semaphore_signal(barrier, inc=1, device_id=dev, device_id_type=MESH)
    pl.semaphore_wait(barrier, len(peers))

    nxt = (ctx + 1) % (QUAD * RING)
    send(proj.at[pl.ds(1, 2), pl.ds(length - RIM, RIM), :], rim, rim_s.at[0], rim_r.at[0], at(nxt, tp))

    fixed = jnp.logical_and(c == hi, hi == lo)
    moves = jnp.logical_not(fixed)
    wdst = at(z * QUAD + 2 * c + hi, y * 2 + lo)

    def wslot(zz, j):
        return wbuf.at[pl.ds(pl.multiple_of(zz * shard, shard), shard), pl.ds(j * ncol, ncol)]

    def wx_copy(j):
        return rcopy(w.at[:, pl.ds(j * ncol, ncol)], wslot(z, j), wx_s.at[j], wx_r.at[j], wdst)

    def wx_start(j):
        @pl.when(fixed)
        def _():
            pltpu.make_async_copy(w.at[:, pl.ds(j * ncol, ncol)], wslot(z, j), wx_r.at[j]).start()

        @pl.when(moves)
        def _():
            wx_copy(j).start()

    def wz_start(j):
        landed(wslot(z, j), wx_r.at[j])
        send(wslot(z, j), wslot(z, j), wz_s.at[j], wz_r.at[j], up)
        send(wslot(z, j), wslot(z, j), wz_s.at[CHUNKS + j], wz_r.at[CHUNKS + j], down)

    def wz_pass(j):
        landed(wslot(zd, j), wz_r.at[j])
        if j in UPWARD:
            send(wslot(zd, j), wslot(zd, j), w2_s.at[j], w2_r.at[j], up)
        landed(wslot(zu, j), wz_r.at[CHUNKS + j])
        if j not in UPWARD:
            send(wslot(zu, j), wslot(zu, j), w2_s.at[j], w2_r.at[j], down)

    wx_start(0)

    tile = half
    ii = lax.broadcasted_iota(jnp.int32, (tile, tile), 0)
    jj = lax.broadcasted_iota(jnp.int32, (tile, tile), 1)
    anti = jnp.where(ii + jj == tile - 1, 1.0, 0.0).astype(bf16)
    for k in range(kept // tile):
        flipped[:, k * tile : (k + 1) * tile] = jnp.dot(
            filt[:, kept - (k + 1) * tile : kept - k * tile], anti, preferred_element_type=f32
        )
    for g in range(groups_here):
        row = flipped[pl.ds(r * groups_here + g, 1), :]
        base = jnp.concatenate([jnp.zeros((1, half), f32), row, jnp.zeros((1, length), f32)], axis=1)
        base = jnp.broadcast_to(base, (16, base.shape[1]))
        base = pltpu.roll(base, 1, 1, stride=1, stride_axis=0)

        def band(k, carry):
            rolled = pltpu.roll(base, 16 * k, 1).astype(bf16)
            start = pl.multiple_of(16 * k, 16)
            strip[g, pl.ds(start, 16), :] = rolled[:, half:]
            strip[g, pl.ds(half + start, 16), :] = rolled[:, : kept + length]
            return carry

        lax.fori_loop(0, half // 16, band, 0)

    def own_rows(rr):
        return pl.ds(pl.multiple_of(kept + rr * length, length), length)

    def halo_rows(rr):
        return pl.ds(pl.multiple_of(rr * length, length), length)

    def mix_piece(s, dst):
        lanes = pl.ds(pl.multiple_of(flip(s) * piece, piece), piece)
        ktap = [taps[1, pl.ds(j, 1), lanes] for j in range(ktaps)]
        vtap = [taps[2, pl.ds(j, 1), lanes] for j in range(ktaps)]

        def rows(i, carry):
            start = pl.multiple_of(i * rows_step - RIM, 16)
            key = proj[1, pl.ds(start, rows_step + RIM), lanes].astype(f32)
            value = proj[2, pl.ds(start, rows_step + RIM), lanes].astype(f32)
            product = short_conv(key, ktap) * short_conv(value, vtap)
            dst[pl.ds(pl.multiple_of(i * rows_step, 16), rows_step), :] = product.astype(bf16)
            return carry

        lax.fori_loop(1, length // rows_step, rows, 0)
        if s == 2:
            landed(rim, rim_r.at[0])
        key = jnp.concatenate([rim[0, :, lanes], proj[1, pl.ds(0, rows_step), lanes]], axis=0).astype(f32)
        value = jnp.concatenate([rim[1, :, lanes], proj[2, pl.ds(0, rows_step), lanes]], axis=0).astype(f32)
        product = short_conv(key, ktap) * short_conv(value, vtap)
        dst[pl.ds(0, rows_step), :] = product.astype(bf16)

    for s in (2, 3, 1):
        mix_piece(s, mixsend.at[s])
        send(mixsend.at[s], seq.at[own_rows(r), :], mix_s.at[s], mix_r.at[s], at(z * QUAD + flip(s), tp))
    mix_piece(0, seq.at[own_rows(r), :])

    def halo_send(s):
        rr = flip(s)
        send(seq.at[own_rows(rr), :], seq.at[halo_rows(rr), :], halo_s.at[s], halo_r.at[rr], up)

    halo_send(0)

    def qrows(rr):
        return pl.ds(pl.multiple_of(RIM + rr * length, 16), length)

    for s in (2, 3, 1):
        lanes = pl.ds(pl.multiple_of(flip(s) * piece, piece), piece)
        send(proj.at[0, :, lanes], qext.at[qrows(r), :], q_s.at[s], q_r.at[s], at(z * QUAD + flip(s), tp))
    mine = pl.ds(pl.multiple_of(r * piece, piece), piece)
    own_query = pltpu.make_async_copy(proj.at[0, :, mine], qext.at[qrows(r), :], q_r.at[0])
    own_query.start()

    def qrim_copy(s):
        return rcopy(
            proj.at[0, pl.ds(length - RIM, RIM), pl.ds(s * piece, piece)],
            qext.at[pl.ds(0, RIM), :],
            qrim_s.at[s], qrim_r.at[0], at(zu * QUAD + s, tp),
        )

    @pl.when(r == QUAD - 1)
    def _():
        for s in range(QUAD):
            qrim_copy(s).start()

    for j in range(1, CHUNKS):
        wx_start(j)

    for s in (1, 2, 3):
        landed(seq.at[own_rows(flip(s)), :], mix_r.at[s])
        halo_send(s)
    wz_start(0)

    landed(qext.at[pl.ds(0, RIM), :], qrim_r.at[0])
    own_query.wait()
    for s in (1, 2, 3):
        landed(qext.at[qrows(flip(s)), :], q_r.at[s])
    qtap = [taps[0, pl.ds(j, 1), mine] for j in range(ktaps)]

    def query_rows(i, carry):
        start = pl.multiple_of(i * rows_step, 16)
        query = qext[pl.ds(start, rows_step + RIM), :].astype(f32)
        qfeat[pl.ds(start, rows_step), :] = short_conv(query, qtap)
        return carry

    lax.fori_loop(0, QUAD * length // rows_step, query_rows, 0)
    wz_start(1)

    gains = gain[:, mine]

    def aslot(yy, cc, b):
        return abuf.at[yy, cc, pl.ds(b * length, length), :]

    for b in ORDER:
        landed(seq.at[pl.ds(b * length, length), :], halo_r.at[b])
        for g in range(groups_here):
            lanes = slice(g * group_width, (g + 1) * group_width)
            window = seq[b * length : b * length + kept + length, lanes]
            toeplitz = jnp.dot(strip[g], window, preferred_element_type=f32)
            skip = gains[:, lanes] * seq[kept + b * length : kept + (b + 1) * length, lanes].astype(f32)
            query = qfeat[b * length : (b + 1) * length, lanes]
            abuf[y, c, b * length : (b + 1) * length, lanes] = (query * (toeplitz + skip)).astype(bf16)
        send(aslot(y, c, b), aslot(y, c, b), a_s.at[b], a_r.at[b], right)
        send(aslot(y, c, b), aslot(y, c, b), a_s.at[4 + b], a_r.at[4 + b], left)
        send(aslot(y, c, b), aslot(y, c, b), a_s.at[8 + b], p_r.at[b], partner)
        if b == 3:
            wz_pass(0)
        if b == 2:
            wz_start(2)

    def a_pass(b):
        landed(aslot(yd, c, b), a_r.at[b])
        if b % 2 == 1:
            send(aslot(yd, c, b), aslot(yd, c, b), a2_s.at[b], a2_r.at[b], right)
        send(aslot(yd, c, b), aslot(yd, c, b), p_s.at[b], p_r.at[4 + b], partner)
        landed(aslot(yu, c, b), a_r.at[4 + b])
        if b % 2 == 0:
            send(aslot(yu, c, b), aslot(yu, c, b), a2_s.at[b], a2_r.at[b], left)
        send(aslot(yu, c, b), aslot(yu, c, b), p_s.at[4 + b], p_r.at[8 + b], partner)

    def a_last(b):
        landed(aslot(y2, c, b), a2_r.at[b])
        send(aslot(y2, c, b), aslot(y2, c, b), p_s.at[8 + b], p_r.at[12 + b], partner)

    a_pass(3)
    wz_pass(1)
    a_pass(2)
    wz_start(3)
    a_pass(1)
    a_pass(0)
    wz_pass(2)
    for b in ORDER:
        a_last(b)
    for b in ORDER:
        for k, yy in enumerate((y, yd, yu, y2)):
            landed(aslot(yy, 1 - c, b), p_r.at[4 * k + b])

    same = c == hi
    apart = jnp.logical_not(same)
    delta = jnp.where(same, 0, 2)

    def c_copy(s, j):
        d = delta + s // 2
        cols = pl.ds(j * ncol, ncol)
        return rcopy(
            csend.at[s, :, cols], crecv.at[d, :, cols], c_s.at[s * CHUNKS + j],
            c_r.at[d * CHUNKS + j], at(z * QUAD + flip(s), y * 2 + c),
        )

    for j in range(CHUNKS):
        landed(wslot(z2, j), w2_r.at[j])
        cols = slice(j * ncol, (j + 1) * ncol)
        for s in (2, 3, 0, 1):
            rows = pl.ds(pl.multiple_of(flip(s) * length, length), length)
            lhs = jnp.concatenate([abuf[k // 2, k % 2, rows, :] for k in range(2 * RING)], axis=1)
            part = jnp.dot(lhs, wbuf[:, cols], preferred_element_type=f32).astype(bf16)
            csend[s, :, cols] = part
            if s == 0:

                @pl.when(same)
                def _():
                    crecv[0, :, cols] = part

                @pl.when(apart)
                def _():
                    c_copy(0, j).start()

            else:
                c_copy(s, j).start()
        if j == 1:
            wz_pass(3)

    for j in range(CHUNKS):
        cols = slice(j * ncol, (j + 1) * ncol)

        @pl.when(apart)
        def _():
            landed(crecv.at[0, :, cols], c_r.at[j])

        for d in range(1, 4):
            landed(crecv.at[d, :, cols], c_r.at[d * CHUNKS + j])
        total = crecv[0, :, cols].astype(f32)
        for d in range(1, 4):
            total = total + crecv[d, :, cols].astype(f32)
        out[:, cols] = total.astype(bf16)

    for copy in sent:
        copy.wait_send()

    @pl.when(moves)
    def _():
        for j in range(CHUNKS):
            wx_copy(j).wait_send()

    @pl.when(r == QUAD - 1)
    def _():
        for s in range(QUAD):
            qrim_copy(s).wait_send()

    @pl.when(apart)
    def _():
        for j in range(CHUNKS):
            c_copy(0, j).wait_send()

    for j in range(CHUNKS):
        for s in range(1, QUAD):
            c_copy(s, j).wait_send()


def local(projected, short_taps, range_filter, skip_gain, out_weight):
    streams, length, width = projected.shape
    piece = width // QUAD
    groups, kept = range_filter.shape
    groups_here = groups // QUAD
    depth, columns = out_weight.shape
    bf16, f32 = jnp.bfloat16, jnp.float32
    vmem = pl.BlockSpec(memory_space=pltpu.VMEM)
    dma = pltpu.SemaphoreType.DMA
    counts = (1, 1, 4, 4, 4, 1, 4, 4, 4, 4, 4, 4, 8, 8, 4, 4, 12, 8, 4, 4, 12, 16, 16, 16)
    return pl.pallas_call(
        kernel,
        out_shape=jax.ShapeDtypeStruct((length, columns), bf16),
        in_specs=[vmem, vmem, vmem, vmem, pl.BlockSpec(memory_space=pl.ANY)],
        out_specs=vmem,
        scratch_shapes=[
            pltpu.VMEM((2, RIM, width), bf16),
            pltpu.VMEM((RIM + QUAD * length, piece), bf16),
            pltpu.VMEM((QUAD * length, piece), f32),
            pltpu.VMEM((QUAD, length, piece), bf16),
            pltpu.VMEM((kept + QUAD * length, piece), bf16),
            pltpu.VMEM((groups, kept), f32),
            pltpu.VMEM((groups_here, length, kept + length), bf16),
            pltpu.VMEM((RING, 2, QUAD * length, piece), bf16),
            pltpu.VMEM((RING * depth, columns), bf16),
            pltpu.VMEM((QUAD, length, columns), bf16),
            pltpu.VMEM((4, length, columns), bf16),
        ]
        + [dma((n,)) for n in counts],
        compiler_params=pltpu.CompilerParams(
            collective_id=0, has_side_effects=True, vmem_limit_bytes=48 * 1024 * 1024
        ),
    )(projected, short_taps, range_filter, skip_gain[None, :], out_weight)


def solution(mesh):
    placed = (P(None, "ctx", "tp"), P(None, None, "tp"), P("tp", None), P("tp"), P("ctx", "tp"))
    return jax.shard_map(
        local, mesh=mesh, in_specs=placed, out_specs=P("ctx", "tp"), check_vma=False
    )
```

```python
import functools

import jax
import jax.numpy as jnp
from jax import lax
from jax.experimental import pallas as pl
from jax.experimental.pallas import tpu as pltpu
from jax.sharding import PartitionSpec as P

MESH = pl.DeviceIdType.MESH
RIM = 16
CUTS = ((0, 4), (4, 4), (8, 4), (12, 2), (14, 2))
CHUNKS = len(CUTS)
RING = 4
QUAD = 4
UPWARD = (2, 4)
ORDER = (3, 1, 2, 0)


def short_conv(extended, tap_rows):
    acc = tap_rows[0] * extended[RIM:]
    for lag in range(1, len(tap_rows)):
        acc = acc + tap_rows[lag] * pltpu.roll(extended, lag, axis=0)[RIM:]
    return acc


def kernel(
    proj, taps_in, filt_in, gain_in, w, out,
    taps, filt, gain, streams, local_s, rim, qext, tsum, mixsend, seq, flipped, strip, abuf, wbuf, csend, crecv,
    rim_s, rim_r, q_s, q_r, qrim_s, qrim_r, mix_s, mix_r, halo_s, halo_r,
    wx_s, wx_r, wz_s, wz_r, w2_s, w2_r, a_s, a_r, a2_s, a2_r, p_s, p_r, c_s, c_r,
):
    length = proj.shape[1]
    piece = proj.shape[2] // QUAD
    ktaps = taps.shape[1]
    groups_here = strip.shape[0]
    group_width = piece // groups_here
    kept = filt.shape[1]
    shard = w.shape[0]
    unit = w.shape[1] // 16
    half = length // 2
    rows_step = length // 4
    f32, bf16 = jnp.float32, jnp.bfloat16

    ctx, tp = lax.axis_index("ctx"), lax.axis_index("tp")
    z, r = ctx // QUAD, ctx % QUAD
    lo, c = r // 2, r % 2
    y, hi = tp // 2, tp % 2
    zu, zd = (z + 1) % RING, (z + RING - 1) % RING
    yu, yd = (y + 1) % RING, (y + RING - 1) % RING
    z2, y2 = (z + 2) % RING, (y + 2) % RING

    def cut(j):
        return pl.ds(CUTS[j][0] * unit, CUTS[j][1] * unit)

    def flip(s):
        b1 = 1 - lo if s & 2 else lo
        b0 = 1 - c if s & 1 else c
        return 2 * b1 + b0

    def at(ctx_, tp_):
        return {"ctx": ctx_, "tp": tp_}

    up, down = at(zu * QUAD + r, tp), at(zd * QUAD + r, tp)
    right, left = at(ctx, yu * 2 + hi), at(ctx, yd * 2 + hi)
    partner = at(z * QUAD + flip(1), tp)

    def rcopy(src, dst, ssem, rsem, dev):
        return pltpu.make_async_remote_copy(
            src_ref=src, dst_ref=dst, send_sem=ssem, recv_sem=rsem, device_id=dev, device_id_type=MESH
        )

    def landed(dst, rsem):
        pltpu.make_async_copy(dst, dst, rsem).wait()

    sent = []

    def send(src, dst, ssem, rsem, dev):
        copy = rcopy(src, dst, ssem, rsem, dev)
        copy.start()
        sent.append(copy)

    barrier = pltpu.get_barrier_semaphore()
    peers = [at(z * QUAD + flip(s), tp) for s in range(1, QUAD)]
    peers += [at(z * QUAD + s, y * 2 + 1 - hi) for s in range(QUAD)]
    peers += [at(zz * QUAD + s, tp) for zz in (zu, zd) for s in range(QUAD)]
    peers += [right, left]
    for dev in peers:
        pl.semaphore_signal(barrier, inc=1, device_id=dev, device_id_type=MESH)
    mine = pl.ds(pl.multiple_of(r * piece, piece), piece)

    def qrows(rr):
        return pl.ds(pl.multiple_of(RIM + rr * length, 16), length)

    loads = [
        pltpu.make_async_copy(src, dst, local_s.at[k])
        for k, (src, dst) in enumerate((
            (taps_in, taps), (proj.at[pl.ds(1, 2)], streams), (filt_in, filt), (gain_in, gain),
            (proj.at[0, :, mine], qext.at[qrows(r), :]),
        ))
    ]
    for load in loads:
        load.start()

    fixed = jnp.logical_and(c == hi, hi == lo)
    moves = jnp.logical_not(fixed)
    wdst = at(z * QUAD + 2 * c + hi, y * 2 + lo)

    def wslot(zz, j):
        return wbuf.at[pl.ds(pl.multiple_of(zz * shard, shard), shard), cut(j)]

    def wx_copy(j):
        return rcopy(w.at[:, cut(j)], wslot(z, j), wx_s.at[j], wx_r.at[j], wdst)

    def wx_start(j):
        @pl.when(fixed)
        def _():
            pltpu.make_async_copy(w.at[:, cut(j)], wslot(z, j), wx_r.at[j]).start()

        @pl.when(moves)
        def _():
            wx_copy(j).start()

    def wz_down(j):
        landed(wslot(z, j), wx_r.at[j])
        send(wslot(z, j), wslot(z, j), wz_s.at[CHUNKS + j], wz_r.at[CHUNKS + j], down)

    def wz_up(j):
        send(wslot(z, j), wslot(z, j), wz_s.at[j], wz_r.at[j], up)

    def from_below(j):
        landed(wslot(zd, j), wz_r.at[j])
        if j in UPWARD:
            send(wslot(zd, j), wslot(zd, j), w2_s.at[j], w2_r.at[j], up)

    def from_above(j):
        landed(wslot(zu, j), wz_r.at[CHUNKS + j])
        if j not in UPWARD:
            send(wslot(zu, j), wslot(zu, j), w2_s.at[j], w2_r.at[j], down)

    def own_rows(rr):
        return pl.ds(pl.multiple_of(kept + rr * length, length), length)

    def halo_rows(rr):
        return pl.ds(pl.multiple_of(rr * length, length), length)

    def mix_dst(s):
        return mixsend.at[s] if s else seq.at[own_rows(r), :]

    def piece_taps(s):
        lanes = pl.ds(pl.multiple_of(flip(s) * piece, piece), piece)
        return lanes, [[taps[m, pl.ds(j, 1), lanes] for j in range(ktaps)] for m in (1, 2)]

    def mix_body(s):
        lanes, (ktap, vtap) = piece_taps(s)
        dst = mix_dst(s)

        def rows(i, carry):
            start = pl.multiple_of(i * rows_step - RIM, 16)
            key = streams[0, pl.ds(start, rows_step + RIM), lanes].astype(f32)
            value = streams[1, pl.ds(start, rows_step + RIM), lanes].astype(f32)
            product = short_conv(key, ktap) * short_conv(value, vtap)
            dst[pl.ds(pl.multiple_of(i * rows_step, 16), rows_step), :] = product.astype(bf16)
            return carry

        lax.fori_loop(1, length // rows_step, rows, 0)

    def mix_head(s):
        lanes, (ktap, vtap) = piece_taps(s)
        key = jnp.concatenate([rim[0, :, lanes], streams[0, pl.ds(0, rows_step), lanes]], axis=0).astype(f32)
        value = jnp.concatenate([rim[1, :, lanes], streams[1, pl.ds(0, rows_step), lanes]], axis=0).astype(f32)
        product = short_conv(key, ktap) * short_conv(value, vtap)
        mix_dst(s)[pl.ds(0, rows_step), :] = product.astype(bf16)

    for load in loads[:2]:
        load.wait()
    for s in (2, 3, 1, 0):
        mix_body(s)

    pl.semaphore_wait(barrier, len(peers))

    nxt = (ctx + 1) % (QUAD * RING)
    send(proj.at[pl.ds(1, 2), pl.ds(length - RIM, RIM), :], rim, rim_s.at[0], rim_r.at[0], at(nxt, tp))

    def qrim_copy(s):
        return rcopy(
            proj.at[0, pl.ds(length - RIM, RIM), pl.ds(s * piece, piece)],
            qext.at[pl.ds(0, RIM), :],
            qrim_s.at[s], qrim_r.at[0], at(zu * QUAD + s, tp),
        )

    @pl.when(r == QUAD - 1)
    def _():
        for s in range(QUAD):
            qrim_copy(s).start()

    parts = (pl.ds(rows_step, length - rows_step), pl.ds(0, rows_step))

    def own_part_rows(rr, part):
        low, size = (rows_step, length - rows_step) if part == 0 else (0, rows_step)
        return pl.ds(pl.multiple_of(kept + rr * length + low, 16), size)

    def halo_part_rows(rr, part):
        low, size = (rows_step, length - rows_step) if part == 0 else (0, rows_step)
        return pl.ds(pl.multiple_of(rr * length + low, 16), size)

    def mix_send(s, part):
        send(
            mixsend.at[s, parts[part], :], seq.at[own_part_rows(r, part), :],
            mix_s.at[2 * s + part], mix_r.at[2 * s + part], at(z * QUAD + flip(s), tp),
        )

    def halo_send(s, part):
        rr = flip(s)
        send(
            seq.at[own_part_rows(rr, part), :], seq.at[halo_part_rows(rr, part), :],
            halo_s.at[2 * s + part], halo_r.at[2 * rr + part], up,
        )

    def mix_pass(s, part):
        landed(seq.at[own_part_rows(flip(s), part), :], mix_r.at[2 * s + part])
        halo_send(s, part)

    wx_start(0)
    for s in (2, 3, 1):
        mix_send(s, 0)
    halo_send(0, 0)

    loads[2].wait()
    tile = half
    ii = lax.broadcasted_iota(jnp.int32, (tile, tile), 0)
    jj = lax.broadcasted_iota(jnp.int32, (tile, tile), 1)
    anti = jnp.where(ii + jj == tile - 1, 1.0, 0.0).astype(bf16)
    ntile = kept // tile
    wide = filt[...].astype(f32)
    stacked = jnp.concatenate([wide[:, k * tile : (k + 1) * tile] for k in range(ntile)], axis=0)
    turned = jnp.dot(stacked.astype(bf16), anti, preferred_element_type=f32)
    rows8 = filt.shape[0]
    for k in range(ntile):
        flipped[:, (ntile - 1 - k) * tile : (ntile - k) * tile] = turned[k * rows8 : (k + 1) * rows8]
    for g in range(groups_here):
        row = flipped[pl.ds(r * groups_here + g, 1), :]
        base = jnp.concatenate([jnp.zeros((1, half), f32), row, jnp.zeros((1, length), f32)], axis=1)
        base = jnp.broadcast_to(base, (16, base.shape[1]))
        base = pltpu.roll(base, 1, 1, stride=1, stride_axis=0)

        def band(k, carry):
            rolled = pltpu.roll(base, 16 * k, 1).astype(bf16)
            start = pl.multiple_of(16 * k, 16)
            strip[g, pl.ds(start, 16), :] = rolled[:, half:]
            strip[g, pl.ds(half + start, 16), :] = rolled[:, : kept + length]
            return carry

        lax.fori_loop(0, half // 16, band, 0)

    landed(rim, rim_r.at[0])
    for s in (2, 3, 1):
        mix_head(s)
        mix_send(s, 1)
    mix_head(0)
    halo_send(0, 1)
    wx_start(1)

    for s in (2, 3, 1):
        lanes = pl.ds(pl.multiple_of(flip(s) * piece, piece), piece)
        send(proj.at[0, :, lanes], qext.at[qrows(r), :], q_s.at[s], q_r.at[s], at(z * QUAD + flip(s), tp))
    for j in range(2, CHUNKS):
        wx_start(j)

    mix_pass(1, 0)
    mix_pass(1, 1)
    mix_pass(2, 0)
    mix_pass(3, 0)
    wz_down(0)
    for s in (2, 3):
        mix_pass(s, 1)
    wz_up(0)

    loads[3].wait()
    gains = gain[:, mine]
    for b in range(QUAD - 1, -1, -1):
        for part in (0, 1):
            landed(seq.at[halo_part_rows(b, part), :], halo_r.at[2 * b + part])
        for g in range(groups_here):
            lanes = slice(g * group_width, (g + 1) * group_width)
            window = seq[b * length : b * length + kept + length, lanes]
            toeplitz = jnp.dot(strip[g], window, preferred_element_type=f32)
            skip = gains[:, lanes] * seq[kept + b * length : kept + (b + 1) * length, lanes].astype(f32)
            tsum[b * length : (b + 1) * length, lanes] = toeplitz + skip

    wz_down(1)
    wz_up(1)

    landed(qext.at[pl.ds(0, RIM), :], qrim_r.at[0])
    loads[4].wait()
    for s in (1, 2, 3):
        landed(qext.at[qrows(flip(s)), :], q_r.at[s])
    qtap = [taps[0, pl.ds(j, 1), mine] for j in range(ktaps)]

    def aslot(yy, cc, b):
        return abuf.at[yy, cc, pl.ds(b * length, length), :]

    def gate(b):
        def gate_rows(i, carry):
            start = pl.multiple_of(b * length + i * rows_step, 16)
            query = short_conv(qext[pl.ds(start, rows_step + RIM), :].astype(f32), qtap)
            abuf[y, c, pl.ds(start, rows_step), :] = (query * tsum[pl.ds(start, rows_step), :]).astype(bf16)
            return carry

        lax.fori_loop(0, length // rows_step, gate_rows, 0)

    def a_send(b):
        gate(b)
        send(aslot(y, c, b), aslot(y, c, b), a_s.at[b], a_r.at[b], right)
        send(aslot(y, c, b), aslot(y, c, b), a_s.at[4 + b], a_r.at[4 + b], left)
        send(aslot(y, c, b), aslot(y, c, b), a_s.at[8 + b], p_r.at[b], partner)

    def a_pass(b):
        landed(aslot(yd, c, b), a_r.at[b])
        if b >= 2:
            send(aslot(yd, c, b), aslot(yd, c, b), a2_s.at[b], a2_r.at[b], right)
        send(aslot(yd, c, b), aslot(yd, c, b), p_s.at[b], p_r.at[4 + b], partner)
        landed(aslot(yu, c, b), a_r.at[4 + b])
        if b < 2:
            send(aslot(yu, c, b), aslot(yu, c, b), a2_s.at[b], a2_r.at[b], left)
        send(aslot(yu, c, b), aslot(yu, c, b), p_s.at[4 + b], p_r.at[8 + b], partner)

    def a_last(b):
        landed(aslot(y2, c, b), a2_r.at[b])
        send(aslot(y2, c, b), aslot(y2, c, b), p_s.at[8 + b], p_r.at[12 + b], partner)

    same = c == hi
    apart = jnp.logical_not(same)
    delta = jnp.where(same, 0, 2)

    def c_copy(b, j):
        d = delta + (1 - lo if b >= 2 else lo)
        cols = cut(j)
        return rcopy(
            csend.at[b, :, cols], crecv.at[d, :, cols], c_s.at[b * CHUNKS + j],
            c_r.at[d * CHUNKS + j], at(z * QUAD + b, y * 2 + c),
        )

    def own_part(b):
        return jnp.logical_and(same, r == b)

    def c_step(b, j):
        cols = cut(j)
        lhs = jnp.concatenate(
            [abuf[k // 2, k % 2, b * length : (b + 1) * length, :] for k in range(2 * RING)], axis=1
        )
        part = jnp.dot(lhs, wbuf[:, cols], preferred_element_type=f32).astype(bf16)
        csend[b, :, cols] = part

        @pl.when(own_part(b))
        def _():
            crecv[0, :, cols] = part

        @pl.when(jnp.logical_not(own_part(b)))
        def _():
            c_copy(b, j).start()

    def a_other(b):
        for k, yy in enumerate((y, yd, yu, y2)):
            landed(aslot(yy, 1 - c, b), p_r.at[4 * k + b])

    def finish(j):
        cols = cut(j)

        @pl.when(apart)
        def _():
            landed(crecv.at[0, :, cols], c_r.at[j])

        for d in range(1, 4):
            landed(crecv.at[d, :, cols], c_r.at[d * CHUNKS + j])
        total = crecv[0, :, cols].astype(f32)
        for d in range(1, 4):
            total = total + crecv[d, :, cols].astype(f32)
        out[:, cols] = total.astype(bf16)

    first, second, third, fourth = ORDER

    def w_ready(j):
        landed(wslot(z2, j), w2_r.at[j])

    a_send(first)
    a_send(second)
    from_above(0)
    a_pass(first)
    a_send(third)
    from_above(1)
    wz_down(2)
    wz_up(2)
    a_pass(second)
    a_send(fourth)
    for j in (3, 4):
        wz_down(j)
        wz_up(j)
    a_last(first)
    from_below(0)
    w_ready(0)
    a_other(first)
    c_step(first, 0)
    a_pass(third)
    a_last(second)
    a_pass(fourth)
    from_below(2)
    a_other(second)
    c_step(second, 0)
    from_below(1)
    w_ready(1)
    c_step(first, 1)
    c_step(second, 1)
    a_last(third)
    a_last(fourth)
    from_below(4)
    a_other(third)
    c_step(third, 0)
    c_step(third, 1)
    a_other(fourth)
    c_step(fourth, 0)
    c_step(fourth, 1)
    from_above(3)
    from_above(2)
    w_ready(2)
    for b in ORDER:
        c_step(b, 2)
    from_above(4)
    w_ready(4)
    for b in ORDER:
        c_step(b, 4)
    from_below(3)
    w_ready(3)
    for b in ORDER:
        c_step(b, 3)
    finish(0)
    for j in range(1, CHUNKS):
        finish(j)

    for copy in sent:
        copy.wait_send()

    @pl.when(moves)
    def _():
        for j in range(CHUNKS):
            wx_copy(j).wait_send()

    @pl.when(r == QUAD - 1)
    def _():
        for s in range(QUAD):
            qrim_copy(s).wait_send()

    for b in range(QUAD):

        @pl.when(jnp.logical_not(own_part(b)))
        def _():
            for j in range(CHUNKS):
                c_copy(b, j).wait_send()


def local(projected, short_taps, range_filter, skip_gain, out_weight):
    streams, length, width = projected.shape
    piece = width // QUAD
    groups, kept = range_filter.shape
    groups_here = groups // QUAD
    depth, columns = out_weight.shape
    bf16, f32 = jnp.bfloat16, jnp.float32
    hbm = pl.BlockSpec(memory_space=pltpu.HBM)
    dma = pltpu.SemaphoreType.DMA
    nc = CHUNKS
    counts = (1, 1, 4, 4, 4, 1, 8, 8, 8, 8, nc, nc, 2 * nc, 2 * nc, nc, nc, 12, 8, 4, 4, 12, 16, 4 * nc, 4 * nc)
    return pl.pallas_call(
        kernel,
        out_shape=jax.ShapeDtypeStruct((length, columns), bf16),
        in_specs=[hbm] * 5,
        out_specs=pl.BlockSpec(memory_space=pltpu.VMEM),
        scratch_shapes=[
            pltpu.VMEM(short_taps.shape, f32),
            pltpu.VMEM((groups, kept), bf16),
            pltpu.VMEM((1, width), f32),
            pltpu.VMEM((2, length, width), bf16),
            dma((5,)),
            pltpu.VMEM((2, RIM, width), bf16),
            pltpu.VMEM((RIM + QUAD * length, piece), bf16),
            pltpu.VMEM((QUAD * length, piece), f32),
            pltpu.VMEM((QUAD, length, piece), bf16),
            pltpu.VMEM((kept + QUAD * length, piece), bf16),
            pltpu.VMEM((groups, kept), f32),
            pltpu.VMEM((groups_here, length, kept + length), bf16),
            pltpu.VMEM((RING, 2, QUAD * length, piece), bf16),
            pltpu.VMEM((RING * depth, columns), bf16),
            pltpu.VMEM((QUAD, length, columns), bf16),
            pltpu.VMEM((4, length, columns), bf16),
        ]
        + [dma((n,)) for n in counts],
        compiler_params=pltpu.CompilerParams(
            collective_id=0, has_side_effects=True, vmem_limit_bytes=50 * 1024 * 1024
        ),
    )(*[pltpu.with_memory_space_constraint(v, pltpu.HBM) for v in (projected, short_taps, range_filter, skip_gain[None, :], out_weight)])


def solution(mesh):
    placed = (P(None, "ctx", "tp"), P(None, None, "tp"), P("tp", None), P("tp"), P("ctx", "tp"))
    return jax.shard_map(
        local, mesh=mesh, in_specs=placed, out_specs=P("ctx", "tp"), check_vma=False
    )
```

```python
import functools

import jax
import jax.numpy as jnp
from jax import lax
from jax.experimental import pallas as pl
from jax.experimental.pallas import tpu as pltpu
from jax.sharding import PartitionSpec as P

MESH = pl.DeviceIdType.MESH
RIM = 16
CUTS = ((0, 4), (4, 4), (8, 4), (12, 2), (14, 2))
CHUNKS = len(CUTS)
TO_RIM, TO_QRIM, TO_MIX, TO_HALO, TO_X, TO_Z, TO_A, TO_C = range(8)
RING = 4
QUAD = 4
UPWARD = (2, 3, 4)
ORDER = (3, 1, 2, 0)


def short_conv(extended, tap_rows):
    acc = tap_rows[0] * extended[RIM:]
    for lag in range(1, len(tap_rows)):
        acc = acc + tap_rows[lag] * pltpu.roll(extended, lag, axis=0)[RIM:]
    return acc


def kernel(
    proj, taps_in, filt_in, gain_in, w, out,
    taps, filt, gain, streams, local_s, rim, qext, tsum, mixsend, seq, flipped, strip, abuf, wbuf, csend, crecv,
    sends, rim_r, q_r, qrim_r, mix_r, halo_r, wx_r, wz_r, w2_r, a_r, a2_r, p_r, c_r,
):
    length = proj.shape[1]
    piece = proj.shape[2] // QUAD
    ktaps = taps.shape[1]
    groups_here = strip.shape[0]
    group_width = piece // groups_here
    kept = filt.shape[1]
    shard = w.shape[0]
    unit = w.shape[1] // 16
    half = length // 2
    rows_step = length // 4
    f32, bf16 = jnp.float32, jnp.bfloat16

    ctx, tp = lax.axis_index("ctx"), lax.axis_index("tp")
    z, r = ctx // QUAD, ctx % QUAD
    lo, c = r // 2, r % 2
    y, hi = tp // 2, tp % 2
    zu, zd = (z + 1) % RING, (z + RING - 1) % RING
    yu, yd = (y + 1) % RING, (y + RING - 1) % RING
    z2, y2 = (z + 2) % RING, (y + 2) % RING

    def cut(j):
        return pl.ds(CUTS[j][0] * unit, CUTS[j][1] * unit)

    def flip(s):
        b1 = 1 - lo if s & 2 else lo
        b0 = 1 - c if s & 1 else c
        return 2 * b1 + b0

    def at(ctx_, tp_):
        return {"ctx": ctx_, "tp": tp_}

    up, down = at(zu * QUAD + r, tp), at(zd * QUAD + r, tp)
    right, left = at(ctx, yu * 2 + hi), at(ctx, yd * 2 + hi)
    partner = at(z * QUAD + flip(1), tp)

    def rcopy(src, dst, ssem, rsem, dev):
        return pltpu.make_async_remote_copy(
            src_ref=src, dst_ref=dst, send_sem=ssem, recv_sem=rsem, device_id=dev, device_id_type=MESH
        )

    def landed(dst, rsem):
        pltpu.make_async_copy(dst, dst, rsem).wait()

    def send(src, dst, kind, rsem, dev):
        rcopy(src, dst, sends.at[kind], rsem, dev).start()

    barrier = pltpu.get_barrier_semaphore()
    peers = [at(z * QUAD + flip(s), tp) for s in range(1, QUAD)]
    peers += [at(z * QUAD + s, y * 2 + 1 - hi) for s in range(QUAD)]
    peers += [at(zz * QUAD + s, tp) for zz in (zu, zd) for s in range(QUAD)]
    peers += [right, left]
    for dev in peers:
        pl.semaphore_signal(barrier, inc=1, device_id=dev, device_id_type=MESH)
    mine = pl.ds(pl.multiple_of(r * piece, piece), piece)

    def qrows(rr):
        return pl.ds(pl.multiple_of(RIM + rr * length, 16), length)

    loads = [
        pltpu.make_async_copy(src, dst, q_r.at[0] if k == 4 else local_s.at[k])
        for k, (src, dst) in enumerate((
            (taps_in, taps), (proj.at[pl.ds(1, 2)], streams), (filt_in, filt), (gain_in, gain),
            (proj.at[0, :, mine], qext.at[qrows(r), :]),
        ))
    ]
    for load in loads:
        load.start()

    fixed = jnp.logical_and(c == hi, hi == lo)
    moves = jnp.logical_not(fixed)
    wdst = at(z * QUAD + 2 * c + hi, y * 2 + lo)

    def wslot(zz, j):
        return wbuf[j].at[pl.ds(pl.multiple_of(zz * shard, shard), shard), :]

    def wx_copy(j):
        return rcopy(w.at[:, cut(j)], wslot(z, j), sends.at[TO_X], wx_r.at[j], wdst)

    def wx_start(j):
        @pl.when(moves)
        def _():
            wx_copy(j).start()

    def z_copy(j, src, upward):
        if upward:
            return rcopy(src, wslot(z, j), sends.at[TO_Z], wz_r.at[j], up)
        return rcopy(src, wslot(z, j), sends.at[TO_Z], wz_r.at[CHUNKS + j], down)

    def fixed_start(upward):
        @pl.when(fixed)
        def _():
            for j in range(CHUNKS):
                if not upward:
                    pltpu.make_async_copy(w.at[:, cut(j)], wslot(z, j), wx_r.at[j]).start()
                z_copy(j, w.at[:, cut(j)], upward).start()

    def wz_down(j):
        landed(wslot(z, j), wx_r.at[j])

        @pl.when(moves)
        def _():
            z_copy(j, wslot(z, j), False).start()

    def wz_up(j):
        @pl.when(moves)
        def _():
            z_copy(j, wslot(z, j), True).start()

    def from_below(j):
        landed(wslot(zd, j), wz_r.at[j])
        if j in UPWARD:
            send(wslot(zd, j), wslot(zd, j), TO_Z, w2_r.at[j], up)

    def from_above(j):
        landed(wslot(zu, j), wz_r.at[CHUNKS + j])
        if j not in UPWARD:
            send(wslot(zu, j), wslot(zu, j), TO_Z, w2_r.at[j], down)

    def own_rows(rr):
        return pl.ds(pl.multiple_of(kept + rr * length, length), length)

    def halo_rows(rr):
        return pl.ds(pl.multiple_of(rr * length, length), length)

    def mix_dst(s):
        return mixsend.at[s] if s else seq.at[own_rows(r), :]

    def piece_taps(s):
        lanes = pl.ds(pl.multiple_of(flip(s) * piece, piece), piece)
        return lanes, [[taps[m, pl.ds(j, 1), lanes] for j in range(ktaps)] for m in (1, 2)]

    def mix_body(s):
        lanes, (ktap, vtap) = piece_taps(s)
        dst = mix_dst(s)

        def rows(i, carry):
            start = pl.multiple_of(i * rows_step - RIM, 16)
            key = streams[0, pl.ds(start, rows_step + RIM), lanes].astype(f32)
            value = streams[1, pl.ds(start, rows_step + RIM), lanes].astype(f32)
            product = short_conv(key, ktap) * short_conv(value, vtap)
            dst[pl.ds(pl.multiple_of(i * rows_step, 16), rows_step), :] = product.astype(bf16)
            return carry

        lax.fori_loop(1, length // rows_step, rows, 0)

    def mix_head(s):
        lanes, (ktap, vtap) = piece_taps(s)
        key = jnp.concatenate([rim[0, :, lanes], streams[0, pl.ds(0, rows_step), lanes]], axis=0).astype(f32)
        value = jnp.concatenate([rim[1, :, lanes], streams[1, pl.ds(0, rows_step), lanes]], axis=0).astype(f32)
        product = short_conv(key, ktap) * short_conv(value, vtap)
        mix_dst(s)[pl.ds(0, rows_step), :] = product.astype(bf16)

    for load in loads[:2]:
        load.wait()
    for s in (2, 3, 1, 0):
        mix_body(s)

    pl.semaphore_wait(barrier, len(peers))

    nxt = (ctx + 1) % (QUAD * RING)
    send(proj.at[pl.ds(1, 2), pl.ds(length - RIM, RIM), :], rim, TO_RIM, rim_r.at[0], at(nxt, tp))

    def qrim_copy(s):
        return rcopy(
            proj.at[0, pl.ds(length - RIM, RIM), pl.ds(s * piece, piece)],
            qext.at[pl.ds(0, RIM), :],
            sends.at[TO_QRIM], qrim_r.at[0], at(zu * QUAD + s, tp),
        )

    @pl.when(r == QUAD - 1)
    def _():
        for s in range(QUAD):
            qrim_copy(s).start()

    parts = (pl.ds(rows_step, length - rows_step), pl.ds(0, rows_step))

    def own_part_rows(rr, part):
        low, size = (rows_step, length - rows_step) if part == 0 else (0, rows_step)
        return pl.ds(pl.multiple_of(kept + rr * length + low, 16), size)

    def halo_part_rows(rr, part):
        low, size = (rows_step, length - rows_step) if part == 0 else (0, rows_step)
        return pl.ds(pl.multiple_of(rr * length + low, 16), size)

    def mix_send(s, part):
        send(
            mixsend.at[s, parts[part], :], seq.at[own_part_rows(r, part), :],
            TO_MIX, mix_r.at[2 * s + part], at(z * QUAD + flip(s), tp),
        )

    def halo_send(s, part):
        rr = flip(s)
        send(
            seq.at[own_part_rows(rr, part), :], seq.at[halo_part_rows(rr, part), :],
            TO_HALO, halo_r.at[rr], up,
        )

    def mix_pass(s, part):
        landed(seq.at[own_part_rows(flip(s), part), :], mix_r.at[2 * s + part])
        halo_send(s, part)

    for s in (2, 3, 1):
        mix_send(s, 0)
    halo_send(0, 0)

    loads[2].wait()
    tile = half
    ii = lax.broadcasted_iota(jnp.int32, (tile, tile), 0)
    jj = lax.broadcasted_iota(jnp.int32, (tile, tile), 1)
    anti = jnp.where(ii + jj == tile - 1, 1.0, 0.0).astype(bf16)
    ntile = kept // tile
    wide = filt[...].astype(f32)
    stacked = jnp.concatenate([wide[:, k * tile : (k + 1) * tile] for k in range(ntile)], axis=0)
    turned = jnp.dot(stacked.astype(bf16), anti, preferred_element_type=f32)
    rows8 = filt.shape[0]
    for k in range(ntile):
        flipped[:, (ntile - 1 - k) * tile : (ntile - k) * tile] = turned[k * rows8 : (k + 1) * rows8]
    for g in range(groups_here):
        row = flipped[pl.ds(r * groups_here + g, 1), :]
        base = jnp.concatenate([jnp.zeros((1, half), f32), row, jnp.zeros((1, length), f32)], axis=1)
        base = jnp.broadcast_to(base, (16, base.shape[1]))
        base = pltpu.roll(base, 1, 1, stride=1, stride_axis=0)

        def band(k, carry):
            rolled = pltpu.roll(base, 16 * k, 1).astype(bf16)
            start = pl.multiple_of(16 * k, 16)
            strip[g, pl.ds(start, 16), :] = rolled[:, half:]
            strip[g, pl.ds(half + start, 16), :] = rolled[:, : kept + length]
            return carry

        lax.fori_loop(0, half // 16, band, 0)

    landed(rim, rim_r.at[0])
    for s in (2, 3, 1):
        mix_head(s)
        mix_send(s, 1)
    mix_head(0)
    halo_send(0, 1)
    wx_start(0)
    fixed_start(False)

    mix_pass(1, 0)
    mix_pass(1, 1)
    mix_pass(2, 0)
    mix_pass(3, 0)
    for s in (2, 3):
        mix_pass(s, 1)

    for s in (2, 3, 1):
        lanes = pl.ds(pl.multiple_of(flip(s) * piece, piece), piece)
        send(proj.at[0, :, lanes], qext.at[qrows(r), :], TO_MIX, q_r.at[0], at(z * QUAD + flip(s), tp))
    for j in range(1, CHUNKS):
        wx_start(j)
    fixed_start(True)
    wz_down(0)
    wz_up(0)

    loads[3].wait()
    gains = gain[:, mine]
    for b in range(QUAD - 1, -1, -1):
        landed(seq.at[pl.ds(b * length, length), :], halo_r.at[b])
        for g in range(groups_here):
            lanes = slice(g * group_width, (g + 1) * group_width)
            window = seq[b * length : b * length + kept + length, lanes]
            toeplitz = jnp.dot(strip[g], window, preferred_element_type=f32)
            skip = gains[:, lanes] * seq[kept + b * length : kept + (b + 1) * length, lanes].astype(f32)
            tsum[b * length : (b + 1) * length, lanes] = toeplitz + skip

    landed(qext.at[pl.ds(0, RIM), :], qrim_r.at[0])
    landed(qext.at[pl.ds(RIM, QUAD * length), :], q_r.at[0])
    qtap = [taps[0, pl.ds(j, 1), mine] for j in range(ktaps)]

    def aslot(yy, cc, b):
        return abuf.at[2 * yy + cc, pl.ds(b * length, length), :]

    def slots(count):
        return abuf.at[pl.ds(0, count)]

    def gate(b):
        def gate_rows(i, carry):
            start = pl.multiple_of(b * length + i * rows_step, 16)
            query = short_conv(qext[pl.ds(start, rows_step + RIM), :].astype(f32), qtap)
            abuf[2 * y + c, pl.ds(start, rows_step), :] = (query * tsum[pl.ds(start, rows_step), :]).astype(bf16)
            return carry

        lax.fori_loop(0, length // rows_step, gate_rows, 0)

    def a_send(b):
        gate(b)
        send(aslot(y, c, b), aslot(y, c, b), TO_A, a_r.at[b], right)
        send(aslot(y, c, b), aslot(y, c, b), TO_A, a_r.at[4 + b], left)
        send(aslot(y, c, b), aslot(y, c, b), TO_A, p_r.at[b], partner)

    def a_pass(b):
        landed(aslot(yd, c, b), a_r.at[b])
        if b >= 2:
            send(aslot(yd, c, b), aslot(yd, c, b), TO_A, a2_r.at[b], right)
        send(aslot(yd, c, b), aslot(yd, c, b), TO_A, p_r.at[b], partner)
        landed(aslot(yu, c, b), a_r.at[4 + b])
        if b < 2:
            send(aslot(yu, c, b), aslot(yu, c, b), TO_A, a2_r.at[b], left)
        send(aslot(yu, c, b), aslot(yu, c, b), TO_A, p_r.at[b], partner)

    def a_last(b):
        landed(aslot(y2, c, b), a2_r.at[b])
        send(aslot(y2, c, b), aslot(y2, c, b), TO_A, p_r.at[b], partner)

    same = c == hi
    apart = jnp.logical_not(same)
    delta = jnp.where(same, 0, 2)

    def c_copy(b, g):
        d = delta + (1 - lo if b >= 2 else lo)
        rsem = c_r.at[jnp.where(d == 0, CHUNKS, 0) + g]
        return rcopy(
            csend[g].at[b], crecv[g].at[d], sends.at[TO_C],
            rsem, at(z * QUAD + b, y * 2 + c),
        )

    def own_part(b):
        return jnp.logical_and(same, r == b)

    def c_step(b, first_group, count=1):
        lhs = jnp.concatenate(
            [abuf[k, b * length : (b + 1) * length, :] for k in range(2 * RING)], axis=1
        )
        groups = range(first_group, first_group + count)
        rhs = wbuf[first_group][...] if count == 1 else jnp.concatenate([wbuf[g][...] for g in groups], axis=1)
        part = jnp.dot(lhs, rhs, preferred_element_type=f32).astype(bf16)
        low = CUTS[first_group][0]
        for g in groups:
            here = part[:, (CUTS[g][0] - low) * unit : (sum(CUTS[g]) - low) * unit]
            csend[g][b] = here

            @pl.when(own_part(b))
            def _():
                crecv[g][0] = here

            @pl.when(jnp.logical_not(own_part(b)))
            def _():
                c_copy(b, g).start()

    def a_other(b):
        landed(slots(1), p_r.at[b])

    def finish(g):
        @pl.when(apart)
        def _():
            landed(crecv[g].at[0], c_r.at[CHUNKS + g])

        landed(crecv[g].at[pl.ds(1, 3)], c_r.at[g])
        total = crecv[g][0].astype(f32)
        for d in range(1, 4):
            total = total + crecv[g][d].astype(f32)
        out[:, cut(g)] = total.astype(bf16)

    first, second, third, fourth = ORDER

    def w_ready(j):
        landed(wslot(z2, j), w2_r.at[j])

    a_send(first)
    a_send(second)
    wz_down(1)
    wz_up(1)
    from_above(0)
    a_pass(first)
    a_send(third)
    from_above(1)
    wz_down(2)
    wz_up(2)
    a_pass(second)
    a_send(fourth)
    for j in (3, 4):
        wz_down(j)
        wz_up(j)
    a_last(first)
    from_below(0)
    w_ready(0)
    a_other(first)
    c_step(first, 0)
    a_pass(third)
    a_last(second)
    a_pass(fourth)
    from_below(2)
    a_other(second)
    c_step(second, 0)
    from_below(1)
    w_ready(1)
    c_step(first, 1)
    c_step(second, 1)
    a_last(third)
    a_last(fourth)
    from_below(3)
    from_below(4)
    a_other(third)
    c_step(third, 0, 2)
    a_other(fourth)
    c_step(fourth, 0, 2)
    for j in range(2, CHUNKS):
        from_above(j)
        if j not in UPWARD:
            from_below(j)
        w_ready(j)
        for b in ORDER:
            c_step(b, j)
    for g in range(CHUNKS):
        finish(g)

    landed(rim, sends.at[TO_RIM])
    landed(seq.at[pl.ds(0, 6 * length), :], sends.at[TO_MIX])
    landed(seq.at[pl.ds(0, 4 * length), :], sends.at[TO_HALO])
    landed(slots(6), sends.at[TO_Z])
    landed(slots(7), sends.at[TO_A])

    @pl.when(moves)
    def _():
        landed(slots(2), sends.at[TO_X])

    @pl.when(r == QUAD - 1)
    def _():
        landed(seq.at[pl.ds(0, QUAD * RIM), :], sends.at[TO_QRIM])

    @pl.when(same)
    def _():
        landed(slots(3), sends.at[TO_C])

    @pl.when(apart)
    def _():
        landed(slots(4), sends.at[TO_C])


def local(projected, short_taps, range_filter, skip_gain, out_weight):
    streams, length, width = projected.shape
    piece = width // QUAD
    groups, kept = range_filter.shape
    groups_here = groups // QUAD
    depth, columns = out_weight.shape
    bf16, f32 = jnp.bfloat16, jnp.float32
    hbm = pl.BlockSpec(memory_space=pltpu.HBM)
    dma = pltpu.SemaphoreType.DMA
    nc = CHUNKS
    widths = [size * columns // 16 for _, size in CUTS]
    counts = (8, 1, 1, 1, 8, 4, nc, 2 * nc, nc, 8, 4, 4, 2 * nc)
    return pl.pallas_call(
        kernel,
        out_shape=jax.ShapeDtypeStruct((length, columns), bf16),
        in_specs=[hbm] * 5,
        out_specs=pl.BlockSpec(memory_space=pltpu.VMEM),
        scratch_shapes=[
            pltpu.VMEM(short_taps.shape, f32),
            pltpu.VMEM((groups, kept), bf16),
            pltpu.VMEM((1, width), f32),
            pltpu.VMEM((2, length, width), bf16),
            dma((5,)),
            pltpu.VMEM((2, RIM, width), bf16),
            pltpu.VMEM((RIM + QUAD * length, piece), bf16),
            pltpu.VMEM((QUAD * length, piece), f32),
            pltpu.VMEM((QUAD, length, piece), bf16),
            pltpu.VMEM((kept + QUAD * length, piece), bf16),
            pltpu.VMEM((groups, kept), f32),
            pltpu.VMEM((groups_here, length, kept + length), bf16),
            pltpu.VMEM((RING * 2, QUAD * length, piece), bf16),
            tuple(pltpu.VMEM((RING * depth, wide), bf16) for wide in widths),
            tuple(pltpu.VMEM((QUAD, length, wide), bf16) for wide in widths),
            tuple(pltpu.VMEM((4, length, wide), bf16) for wide in widths),
        ]
        + [dma((n,)) for n in counts],
        compiler_params=pltpu.CompilerParams(
            collective_id=0, has_side_effects=True, vmem_limit_bytes=50 * 1024 * 1024
        ),
    )(*[pltpu.with_memory_space_constraint(v, pltpu.HBM) for v in (projected, short_taps, range_filter, skip_gain[None, :], out_weight)])


def solution(mesh):
    placed = (P(None, "ctx", "tp"), P(None, None, "tp"), P("tp", None), P("tp"), P("ctx", "tp"))
    return jax.shard_map(
        local, mesh=mesh, in_specs=placed, out_specs=P("ctx", "tp"), check_vma=False
    )
```

```python
import functools

import jax
import jax.numpy as jnp
from jax import lax
from jax.experimental import pallas as pl
from jax.experimental.pallas import tpu as pltpu
from jax.sharding import PartitionSpec as P

MESH = pl.DeviceIdType.MESH
RIM = 16
CUTS = ((0, 4), (4, 4), (8, 4), (12, 2), (14, 2))
CHUNKS = len(CUTS)
TO_RIM, TO_QRIM, TO_MIX, TO_HALO, TO_X, TO_Z, TO_A, TO_C = range(8)
RING = 4
QUAD = 4
UPWARD = (2, 3, 4)
EARLY = (0, 1)
ORDER = (3, 1, 2, 0)


def short_conv(extended, tap_rows):
    acc = tap_rows[0] * extended[RIM:]
    for lag in range(1, len(tap_rows)):
        acc = acc + tap_rows[lag] * pltpu.roll(extended, lag, axis=0)[RIM:]
    return acc


def kernel(
    proj, taps_in, filt_in, gain_in, w, out,
    taps, filt, gain, streams, local_s, rim, qext, tsum, mixsend, seq, flipped, strip, abuf, wbuf, csend, crecv,
    sends, rim_r, q_r, qrim_r, mix_r, halo_r, wx_r, wz_r, w2_r, a_r, a2_r, p_r, c_r,
):
    length = proj.shape[1]
    piece = proj.shape[2] // QUAD
    ktaps = taps.shape[1]
    groups_here = strip.shape[0]
    group_width = piece // groups_here
    kept = filt.shape[1]
    shard = w.shape[0]
    unit = w.shape[1] // 16
    half = length // 2
    rows_step = length // 4
    f32, bf16 = jnp.float32, jnp.bfloat16

    ctx, tp = lax.axis_index("ctx"), lax.axis_index("tp")
    z, r = ctx // QUAD, ctx % QUAD
    lo, c = r // 2, r % 2
    y, hi = tp // 2, tp % 2
    zu, zd = (z + 1) % RING, (z + RING - 1) % RING
    yu, yd = (y + 1) % RING, (y + RING - 1) % RING
    z2, y2 = (z + 2) % RING, (y + 2) % RING

    def cut(j):
        return pl.ds(CUTS[j][0] * unit, CUTS[j][1] * unit)

    def flip(s):
        b1 = 1 - lo if s & 2 else lo
        b0 = 1 - c if s & 1 else c
        return 2 * b1 + b0

    def at(ctx_, tp_):
        return {"ctx": ctx_, "tp": tp_}

    up, down = at(zu * QUAD + r, tp), at(zd * QUAD + r, tp)
    right, left = at(ctx, yu * 2 + hi), at(ctx, yd * 2 + hi)
    partner = at(z * QUAD + flip(1), tp)

    def rcopy(src, dst, ssem, rsem, dev):
        return pltpu.make_async_remote_copy(
            src_ref=src, dst_ref=dst, send_sem=ssem, recv_sem=rsem, device_id=dev, device_id_type=MESH
        )

    def landed(dst, rsem):
        pltpu.make_async_copy(dst, dst, rsem).wait()

    def send(src, dst, kind, rsem, dev):
        rcopy(src, dst, sends.at[kind], rsem, dev).start()

    barrier = pltpu.get_barrier_semaphore()
    peers = [at(z * QUAD + flip(s), tp) for s in range(1, QUAD)]
    peers += [at(z * QUAD + s, y * 2 + 1 - hi) for s in range(QUAD)]
    peers += [at(zz * QUAD + s, tp) for zz in (zu, zd) for s in range(QUAD)]
    peers += [right, left]
    for dev in peers:
        pl.semaphore_signal(barrier, inc=1, device_id=dev, device_id_type=MESH)
    mine = pl.ds(pl.multiple_of(r * piece, piece), piece)

    def qrows(rr):
        return pl.ds(pl.multiple_of(RIM + rr * length, 16), length)

    loads = [
        pltpu.make_async_copy(src, dst, q_r.at[0] if k == 4 else local_s.at[k])
        for k, (src, dst) in enumerate((
            (taps_in, taps), (proj.at[pl.ds(1, 2)], streams), (filt_in, filt), (gain_in, gain),
            (proj.at[0, :, mine], qext.at[qrows(r), :]),
        ))
    ]
    for load in loads:
        load.start()

    fixed = jnp.logical_and(c == hi, hi == lo)
    moves = jnp.logical_not(fixed)
    wdst = at(z * QUAD + 2 * c + hi, y * 2 + lo)

    def wslot(zz, j):
        return wbuf[j].at[pl.ds(pl.multiple_of(zz * shard, shard), shard), :]

    def wx_copy(j):
        return rcopy(w.at[:, cut(j)], wslot(z, j), sends.at[TO_X], wx_r.at[j], wdst)

    soon = jnp.logical_and(lo != hi, c == hi)
    soon_here = jnp.logical_and(lo != hi, c == lo)

    def wx_start(j):
        @pl.when(jnp.logical_and(moves, jnp.logical_not(soon)))
        def _():
            wx_copy(j).start()

    def z_copy(j, src, upward):
        if upward:
            return rcopy(src, wslot(z, j), sends.at[TO_Z], wz_r.at[j], up)
        return rcopy(src, wslot(z, j), sends.at[TO_Z], wz_r.at[CHUNKS + j], down)

    def fixed_start(upward):
        @pl.when(fixed)
        def _():
            for j in range(CHUNKS):
                if not upward:
                    pltpu.make_async_copy(w.at[:, cut(j)], wslot(z, j), wx_r.at[j]).start()
                z_copy(j, w.at[:, cut(j)], upward).start()

    def wz_down(j):
        late = jnp.logical_not(soon_here) if j in EARLY else True

        @pl.when(late)
        def _():
            landed(wslot(z, j), wx_r.at[j])

        @pl.when(jnp.logical_and(moves, late))
        def _():
            z_copy(j, wslot(z, j), False).start()

    def wz_up(j):
        @pl.when(moves)
        def _():
            z_copy(j, wslot(z, j), True).start()

    def from_below(j):
        landed(wslot(zd, j), wz_r.at[j])
        if j in UPWARD:
            send(wslot(zd, j), wslot(zd, j), TO_Z, w2_r.at[j], up)

    def from_above(j):
        landed(wslot(zu, j), wz_r.at[CHUNKS + j])
        if j not in UPWARD:
            send(wslot(zu, j), wslot(zu, j), TO_Z, w2_r.at[j], down)

    def own_rows(rr):
        return pl.ds(pl.multiple_of(kept + rr * length, length), length)

    def halo_rows(rr):
        return pl.ds(pl.multiple_of(rr * length, length), length)

    def mix_dst(s):
        return mixsend.at[s] if s else seq.at[own_rows(r), :]

    def piece_taps(s):
        lanes = pl.ds(pl.multiple_of(flip(s) * piece, piece), piece)
        return lanes, [[taps[m, pl.ds(j, 1), lanes] for j in range(ktaps)] for m in (1, 2)]

    def mix_body(s):
        lanes, (ktap, vtap) = piece_taps(s)
        dst = mix_dst(s)

        def rows(i, carry):
            start = pl.multiple_of(i * rows_step - RIM, 16)
            key = streams[0, pl.ds(start, rows_step + RIM), lanes].astype(f32)
            value = streams[1, pl.ds(start, rows_step + RIM), lanes].astype(f32)
            product = short_conv(key, ktap) * short_conv(value, vtap)
            dst[pl.ds(pl.multiple_of(i * rows_step, 16), rows_step), :] = product.astype(bf16)
            return carry

        lax.fori_loop(1, length // rows_step, rows, 0)

    def mix_head(s):
        lanes, (ktap, vtap) = piece_taps(s)
        key = jnp.concatenate([rim[0, :, lanes], streams[0, pl.ds(0, rows_step), lanes]], axis=0).astype(f32)
        value = jnp.concatenate([rim[1, :, lanes], streams[1, pl.ds(0, rows_step), lanes]], axis=0).astype(f32)
        product = short_conv(key, ktap) * short_conv(value, vtap)
        mix_dst(s)[pl.ds(0, rows_step), :] = product.astype(bf16)

    for load in loads[:2]:
        load.wait()
    for s in (2, 3, 1, 0):
        mix_body(s)

    pl.semaphore_wait(barrier, len(peers))

    nxt = (ctx + 1) % (QUAD * RING)
    send(proj.at[pl.ds(1, 2), pl.ds(length - RIM, RIM), :], rim, TO_RIM, rim_r.at[0], at(nxt, tp))

    def qrim_copy(s):
        return rcopy(
            proj.at[0, pl.ds(length - RIM, RIM), pl.ds(s * piece, piece)],
            qext.at[pl.ds(0, RIM), :],
            sends.at[TO_QRIM], qrim_r.at[0], at(zu * QUAD + s, tp),
        )

    @pl.when(r == QUAD - 1)
    def _():
        for s in range(QUAD):
            qrim_copy(s).start()

    parts = (pl.ds(rows_step, length - rows_step), pl.ds(0, rows_step))

    def own_part_rows(rr, part):
        low, size = (rows_step, length - rows_step) if part == 0 else (0, rows_step)
        return pl.ds(pl.multiple_of(kept + rr * length + low, 16), size)

    def halo_part_rows(rr, part):
        low, size = (rows_step, length - rows_step) if part == 0 else (0, rows_step)
        return pl.ds(pl.multiple_of(rr * length + low, 16), size)

    def mix_send(s, part):
        send(
            mixsend.at[s, parts[part], :], seq.at[own_part_rows(r, part), :],
            TO_MIX, mix_r.at[2 * s + part], at(z * QUAD + flip(s), tp),
        )

    def halo_send(s, part):
        rr = flip(s)
        send(
            seq.at[own_part_rows(rr, part), :], seq.at[halo_part_rows(rr, part), :],
            TO_HALO, halo_r.at[rr], up,
        )

    def mix_pass(s, part):
        landed(seq.at[own_part_rows(flip(s), part), :], mix_r.at[2 * s + part])
        halo_send(s, part)

    @pl.when(soon)
    def _():
        for j in range(CHUNKS):
            wx_copy(j).start()

    for s in (2, 3, 1):
        mix_send(s, 0)
    halo_send(0, 0)

    loads[2].wait()
    tile = half
    ii = lax.broadcasted_iota(jnp.int32, (tile, tile), 0)
    jj = lax.broadcasted_iota(jnp.int32, (tile, tile), 1)
    anti = jnp.where(ii + jj == tile - 1, 1.0, 0.0).astype(bf16)
    ntile = kept // tile
    wide = filt[...].astype(f32)
    stacked = jnp.concatenate([wide[:, k * tile : (k + 1) * tile] for k in range(ntile)], axis=0)
    turned = jnp.dot(stacked.astype(bf16), anti, preferred_element_type=f32)
    rows8 = filt.shape[0]
    for k in range(ntile):
        flipped[:, (ntile - 1 - k) * tile : (ntile - k) * tile] = turned[k * rows8 : (k + 1) * rows8]
    for g in range(groups_here):
        row = flipped[pl.ds(r * groups_here + g, 1), :]
        base = jnp.concatenate([jnp.zeros((1, half), f32), row, jnp.zeros((1, length), f32)], axis=1)
        base = jnp.broadcast_to(base, (16, base.shape[1]))
        base = pltpu.roll(base, 1, 1, stride=1, stride_axis=0)

        def band(k, carry):
            rolled = pltpu.roll(base, 16 * k, 1).astype(bf16)
            start = pl.multiple_of(16 * k, 16)
            strip[g, pl.ds(start, 16), :] = rolled[:, half:]
            strip[g, pl.ds(half + start, 16), :] = rolled[:, : kept + length]
            return carry

        lax.fori_loop(0, half // 16, band, 0)

    landed(rim, rim_r.at[0])
    for s in (2, 3, 1):
        mix_head(s)
        mix_send(s, 1)
    mix_head(0)
    halo_send(0, 1)
    wx_start(0)
    fixed_start(False)

    mix_pass(1, 0)
    mix_pass(1, 1)
    mix_pass(2, 0)
    mix_pass(3, 0)
    for s in (2, 3):
        mix_pass(s, 1)

    @pl.when(soon_here)
    def _():
        for j in EARLY:
            landed(wslot(z, j), wx_r.at[j])
            z_copy(j, wslot(z, j), False).start()

    for s in (2, 3, 1):
        lanes = pl.ds(pl.multiple_of(flip(s) * piece, piece), piece)
        send(proj.at[0, :, lanes], qext.at[qrows(r), :], TO_MIX, q_r.at[0], at(z * QUAD + flip(s), tp))
    for j in range(1, CHUNKS):
        wx_start(j)
    fixed_start(True)
    wz_down(0)
    wz_up(0)

    loads[3].wait()
    gains = gain[:, mine]
    for b in range(QUAD - 1, -1, -1):
        landed(seq.at[pl.ds(b * length, length), :], halo_r.at[b])
        for g in range(groups_here):
            lanes = slice(g * group_width, (g + 1) * group_width)
            window = seq[b * length : b * length + kept + length, lanes]
            toeplitz = jnp.dot(strip[g], window, preferred_element_type=f32)
            skip = gains[:, lanes] * seq[kept + b * length : kept + (b + 1) * length, lanes].astype(f32)
            tsum[b * length : (b + 1) * length, lanes] = toeplitz + skip

    landed(qext.at[pl.ds(0, RIM), :], qrim_r.at[0])
    landed(qext.at[pl.ds(RIM, QUAD * length), :], q_r.at[0])
    qtap = [taps[0, pl.ds(j, 1), mine] for j in range(ktaps)]

    def aslot(yy, cc, b):
        return abuf.at[2 * yy + cc, pl.ds(b * length, length), :]

    def slots(count):
        return abuf.at[pl.ds(0, count)]

    def gate(b):
        def gate_rows(i, carry):
            start = pl.multiple_of(b * length + i * rows_step, 16)
            query = short_conv(qext[pl.ds(start, rows_step + RIM), :].astype(f32), qtap)
            abuf[2 * y + c, pl.ds(start, rows_step), :] = (query * tsum[pl.ds(start, rows_step), :]).astype(bf16)
            return carry

        lax.fori_loop(0, length // rows_step, gate_rows, 0)

    def a_send(b):
        gate(b)
        send(aslot(y, c, b), aslot(y, c, b), TO_A, a_r.at[b], right)
        send(aslot(y, c, b), aslot(y, c, b), TO_A, a_r.at[4 + b], left)
        send(aslot(y, c, b), aslot(y, c, b), TO_A, p_r.at[b], partner)

    def a_pass(b):
        landed(aslot(yd, c, b), a_r.at[b])
        if b >= 2:
            send(aslot(yd, c, b), aslot(yd, c, b), TO_A, a2_r.at[b], right)
        send(aslot(yd, c, b), aslot(yd, c, b), TO_A, p_r.at[b], partner)
        landed(aslot(yu, c, b), a_r.at[4 + b])
        if b < 2:
            send(aslot(yu, c, b), aslot(yu, c, b), TO_A, a2_r.at[b], left)
        send(aslot(yu, c, b), aslot(yu, c, b), TO_A, p_r.at[b], partner)

    def a_last(b):
        landed(aslot(y2, c, b), a2_r.at[b])
        send(aslot(y2, c, b), aslot(y2, c, b), TO_A, p_r.at[b], partner)

    same = c == hi
    apart = jnp.logical_not(same)
    delta = jnp.where(same, 0, 2)

    def c_copy(b, g):
        d = delta + (1 - lo if b >= 2 else lo)
        rsem = c_r.at[jnp.where(d == 0, CHUNKS, 0) + g]
        return rcopy(
            csend[g].at[b], crecv[g].at[d], sends.at[TO_C],
            rsem, at(z * QUAD + b, y * 2 + c),
        )

    def own_part(b):
        return jnp.logical_and(same, r == b)

    def c_step(b, first_group, count=1):
        lhs = jnp.concatenate(
            [abuf[k, b * length : (b + 1) * length, :] for k in range(2 * RING)], axis=1
        )
        groups = range(first_group, first_group + count)
        rhs = wbuf[first_group][...] if count == 1 else jnp.concatenate([wbuf[g][...] for g in groups], axis=1)
        part = jnp.dot(lhs, rhs, preferred_element_type=f32).astype(bf16)
        low = CUTS[first_group][0]
        for g in groups:
            here = part[:, (CUTS[g][0] - low) * unit : (sum(CUTS[g]) - low) * unit]
            csend[g][b] = here

            @pl.when(own_part(b))
            def _():
                crecv[g][0] = here

            @pl.when(jnp.logical_not(own_part(b)))
            def _():
                c_copy(b, g).start()

    def a_other(b):
        landed(slots(1), p_r.at[b])

    def finish(g):
        @pl.when(apart)
        def _():
            landed(crecv[g].at[0], c_r.at[CHUNKS + g])

        landed(crecv[g].at[pl.ds(1, 3)], c_r.at[g])
        total = crecv[g][0].astype(f32)
        for d in range(1, 4):
            total = total + crecv[g][d].astype(f32)
        out[:, cut(g)] = total.astype(bf16)

    first, second, third, fourth = ORDER

    def w_ready(j):
        landed(wslot(z2, j), w2_r.at[j])

    a_send(first)
    a_send(second)
    wz_down(1)
    wz_up(1)
    from_above(0)
    a_pass(first)
    a_send(third)
    from_above(1)
    wz_down(2)
    wz_up(2)
    a_pass(second)
    a_send(fourth)
    for j in (3, 4):
        wz_down(j)
        wz_up(j)
    a_last(first)
    from_below(0)
    w_ready(0)
    a_other(first)
    c_step(first, 0)
    a_pass(third)
    a_last(second)
    a_pass(fourth)
    from_below(2)
    a_other(second)
    c_step(second, 0)
    from_below(1)
    w_ready(1)
    c_step(first, 1)
    c_step(second, 1)
    a_last(third)
    a_last(fourth)
    from_below(3)
    from_below(4)
    a_other(third)
    c_step(third, 0, 2)
    a_other(fourth)
    c_step(fourth, 0, 2)
    for j in range(2, CHUNKS):
        from_above(j)
        if j not in UPWARD:
            from_below(j)
        w_ready(j)
        for b in ORDER:
            c_step(b, j)
    for g in range(CHUNKS):
        finish(g)

    landed(rim, sends.at[TO_RIM])
    landed(seq.at[pl.ds(0, 6 * length), :], sends.at[TO_MIX])
    landed(seq.at[pl.ds(0, 4 * length), :], sends.at[TO_HALO])
    landed(slots(6), sends.at[TO_Z])
    landed(slots(7), sends.at[TO_A])

    @pl.when(moves)
    def _():
        landed(slots(2), sends.at[TO_X])

    @pl.when(r == QUAD - 1)
    def _():
        landed(seq.at[pl.ds(0, QUAD * RIM), :], sends.at[TO_QRIM])

    @pl.when(same)
    def _():
        landed(slots(3), sends.at[TO_C])

    @pl.when(apart)
    def _():
        landed(slots(4), sends.at[TO_C])


def local(projected, short_taps, range_filter, skip_gain, out_weight):
    streams, length, width = projected.shape
    piece = width // QUAD
    groups, kept = range_filter.shape
    groups_here = groups // QUAD
    depth, columns = out_weight.shape
    bf16, f32 = jnp.bfloat16, jnp.float32
    hbm = pl.BlockSpec(memory_space=pltpu.HBM)
    dma = pltpu.SemaphoreType.DMA
    nc = CHUNKS
    widths = [size * columns // 16 for _, size in CUTS]
    counts = (8, 1, 1, 1, 8, 4, nc, 2 * nc, nc, 8, 4, 4, 2 * nc)
    return pl.pallas_call(
        kernel,
        out_shape=jax.ShapeDtypeStruct((length, columns), bf16),
        in_specs=[hbm] * 5,
        out_specs=pl.BlockSpec(memory_space=pltpu.VMEM),
        scratch_shapes=[
            pltpu.VMEM(short_taps.shape, f32),
            pltpu.VMEM((groups, kept), bf16),
            pltpu.VMEM((1, width), f32),
            pltpu.VMEM((2, length, width), bf16),
            dma((5,)),
            pltpu.VMEM((2, RIM, width), bf16),
            pltpu.VMEM((RIM + QUAD * length, piece), bf16),
            pltpu.VMEM((QUAD * length, piece), f32),
            pltpu.VMEM((QUAD, length, piece), bf16),
            pltpu.VMEM((kept + QUAD * length, piece), bf16),
            pltpu.VMEM((groups, kept), f32),
            pltpu.VMEM((groups_here, length, kept + length), bf16),
            pltpu.VMEM((RING * 2, QUAD * length, piece), bf16),
            tuple(pltpu.VMEM((RING * depth, wide), bf16) for wide in widths),
            tuple(pltpu.VMEM((QUAD, length, wide), bf16) for wide in widths),
            tuple(pltpu.VMEM((4, length, wide), bf16) for wide in widths),
        ]
        + [dma((n,)) for n in counts],
        compiler_params=pltpu.CompilerParams(
            collective_id=0, has_side_effects=True, vmem_limit_bytes=50 * 1024 * 1024
        ),
    )(*[pltpu.with_memory_space_constraint(v, pltpu.HBM) for v in (projected, short_taps, range_filter, skip_gain[None, :], out_weight)])


def solution(mesh):
    placed = (P(None, "ctx", "tp"), P(None, None, "tp"), P("tp", None), P("tp"), P("ctx", "tp"))
    return jax.shard_map(
        local, mesh=mesh, in_specs=placed, out_specs=P("ctx", "tp"), check_vma=False
    )
```

```python
import functools

import jax
import jax.numpy as jnp
from jax import lax
from jax.experimental import pallas as pl
from jax.experimental.pallas import tpu as pltpu
from jax.sharding import PartitionSpec as P

MESH = pl.DeviceIdType.MESH
RIM = 16
CUTS = ((0, 4), (4, 4), (8, 4), (12, 2), (14, 2))
CHUNKS = len(CUTS)
TO_RIM, TO_QRIM, TO_MIX, TO_HALO, TO_X, TO_Z, TO_A, TO_C = range(8)
RING = 4
QUAD = 4
UPWARD = (2, 3, 4)
EARLY = (0, 1)
ORDER = (3, 1, 2, 0)


def short_conv(extended, tap_rows):
    acc = tap_rows[0] * extended[RIM:]
    for lag in range(1, len(tap_rows)):
        acc = acc + tap_rows[lag] * pltpu.roll(extended, lag, axis=0)[RIM:]
    return acc


def kernel(
    proj, taps_in, filt_in, gain_in, w, out,
    taps, filt, gain, streams, local_s, rim, qext, tsum, mixsend, seq, flipped, strip, abuf, wbuf, csend, crecv,
    sends, rim_r, q_r, qrim_r, mix_r, halo_r, wx_r, wz_r, w2_r, a_r, a2_r, p_r, c_r,
):
    length = proj.shape[1]
    piece = proj.shape[2] // QUAD
    ktaps = taps.shape[1]
    groups_here = strip.shape[0]
    group_width = piece // groups_here
    kept = filt.shape[1]
    shard = w.shape[0]
    unit = w.shape[1] // 16
    half = length // 2
    rows_step = length // 4
    f32, bf16 = jnp.float32, jnp.bfloat16

    ctx, tp = lax.axis_index("ctx"), lax.axis_index("tp")
    z, r = ctx // QUAD, ctx % QUAD
    lo, c = r // 2, r % 2
    y, hi = tp // 2, tp % 2
    zu, zd = (z + 1) % RING, (z + RING - 1) % RING
    yu, yd = (y + 1) % RING, (y + RING - 1) % RING
    z2, y2 = (z + 2) % RING, (y + 2) % RING

    def cut(j):
        return pl.ds(CUTS[j][0] * unit, CUTS[j][1] * unit)

    def flip(s):
        b1 = 1 - lo if s & 2 else lo
        b0 = 1 - c if s & 1 else c
        return 2 * b1 + b0

    def at(ctx_, tp_):
        return {"ctx": ctx_, "tp": tp_}

    up, down = at(zu * QUAD + r, tp), at(zd * QUAD + r, tp)
    right, left = at(ctx, yu * 2 + hi), at(ctx, yd * 2 + hi)
    partner = at(z * QUAD + flip(1), tp)

    def rcopy(src, dst, ssem, rsem, dev):
        return pltpu.make_async_remote_copy(
            src_ref=src, dst_ref=dst, send_sem=ssem, recv_sem=rsem, device_id=dev, device_id_type=MESH
        )

    def landed(dst, rsem):
        pltpu.make_async_copy(dst, dst, rsem).wait()

    def send(src, dst, kind, rsem, dev):
        rcopy(src, dst, sends.at[kind], rsem, dev).start()

    barrier = pltpu.get_barrier_semaphore()
    peers = [at(z * QUAD + flip(s), tp) for s in range(1, QUAD)]
    peers += [at(z * QUAD + s, y * 2 + 1 - hi) for s in range(QUAD)]
    peers += [at(zz * QUAD + s, tp) for zz in (zu, zd) for s in range(QUAD)]
    peers += [right, left]
    for dev in peers:
        pl.semaphore_signal(barrier, inc=1, device_id=dev, device_id_type=MESH)
    mine = pl.ds(pl.multiple_of(r * piece, piece), piece)

    def qrows(rr):
        return pl.ds(pl.multiple_of(RIM + rr * length, 16), length)

    loads = [
        pltpu.make_async_copy(src, dst, q_r.at[0] if k == 3 else local_s.at[k])
        for k, (src, dst) in enumerate((
            (taps_in, taps), (filt_in, filt), (gain_in, gain),
            (proj.at[0, :, mine], qext.at[qrows(r), :]),
        ))
    ]
    lanes_of = [pl.ds(pl.multiple_of(flip(s) * piece, piece), piece) for s in (2, 3, 1, 0)]
    piece_loads = [
        pltpu.make_async_copy(proj.at[pl.ds(1, 2), :, lanes], streams.at[:, :, lanes], local_s.at[3 + k])
        for k, lanes in enumerate(lanes_of)
    ]
    for load in loads[:1] + piece_loads + loads[1:]:
        load.start()

    fixed = jnp.logical_and(c == hi, hi == lo)
    moves = jnp.logical_not(fixed)
    wdst = at(z * QUAD + 2 * c + hi, y * 2 + lo)

    def wslot(zz, j):
        return wbuf[j].at[pl.ds(pl.multiple_of(zz * shard, shard), shard), :]

    def wx_copy(j):
        return rcopy(w.at[:, cut(j)], wslot(z, j), sends.at[TO_X], wx_r.at[j], wdst)

    soon = jnp.logical_and(lo != hi, c == hi)
    soon_here = jnp.logical_and(lo != hi, c == lo)

    def wx_start(j):
        @pl.when(jnp.logical_and(moves, jnp.logical_not(soon)))
        def _():
            wx_copy(j).start()

    def z_copy(j, src, upward):
        if upward:
            return rcopy(src, wslot(z, j), sends.at[TO_Z], wz_r.at[j], up)
        return rcopy(src, wslot(z, j), sends.at[TO_Z], wz_r.at[CHUNKS + j], down)

    def fixed_start(upward):
        @pl.when(fixed)
        def _():
            for j in range(CHUNKS):
                if not upward:
                    pltpu.make_async_copy(w.at[:, cut(j)], wslot(z, j), wx_r.at[j]).start()
                z_copy(j, w.at[:, cut(j)], upward).start()

    def wz_down(j):
        late = jnp.logical_not(soon_here) if j in EARLY else True

        @pl.when(late)
        def _():
            landed(wslot(z, j), wx_r.at[j])

        @pl.when(jnp.logical_and(moves, late))
        def _():
            z_copy(j, wslot(z, j), False).start()

    def wz_up(j):
        @pl.when(moves)
        def _():
            z_copy(j, wslot(z, j), True).start()

    def from_below(j):
        landed(wslot(zd, j), wz_r.at[j])
        if j in UPWARD:
            send(wslot(zd, j), wslot(zd, j), TO_Z, w2_r.at[j], up)

    def from_above(j):
        landed(wslot(zu, j), wz_r.at[CHUNKS + j])
        if j not in UPWARD:
            send(wslot(zu, j), wslot(zu, j), TO_Z, w2_r.at[j], down)

    def own_rows(rr):
        return pl.ds(pl.multiple_of(kept + rr * length, length), length)

    def halo_rows(rr):
        return pl.ds(pl.multiple_of(rr * length, length), length)

    def mix_dst(s):
        return mixsend.at[s] if s else seq.at[own_rows(r), :]

    def piece_taps(s):
        lanes = pl.ds(pl.multiple_of(flip(s) * piece, piece), piece)
        return lanes, [[taps[m, pl.ds(j, 1), lanes] for j in range(ktaps)] for m in (1, 2)]

    def mix_body(s):
        lanes, (ktap, vtap) = piece_taps(s)
        dst = mix_dst(s)

        def rows(i, carry):
            start = pl.multiple_of(i * rows_step - RIM, 16)
            key = streams[0, pl.ds(start, rows_step + RIM), lanes].astype(f32)
            value = streams[1, pl.ds(start, rows_step + RIM), lanes].astype(f32)
            product = short_conv(key, ktap) * short_conv(value, vtap)
            dst[pl.ds(pl.multiple_of(i * rows_step, 16), rows_step), :] = product.astype(bf16)
            return carry

        lax.fori_loop(1, length // rows_step, rows, 0)

    def mix_head(s):
        lanes, (ktap, vtap) = piece_taps(s)
        key = jnp.concatenate([rim[0, :, lanes], streams[0, pl.ds(0, rows_step), lanes]], axis=0).astype(f32)
        value = jnp.concatenate([rim[1, :, lanes], streams[1, pl.ds(0, rows_step), lanes]], axis=0).astype(f32)
        product = short_conv(key, ktap) * short_conv(value, vtap)
        mix_dst(s)[pl.ds(0, rows_step), :] = product.astype(bf16)

    loads[0].wait()
    for k, s in enumerate((2, 3)):
        piece_loads[k].wait()
        mix_body(s)

    pl.semaphore_wait(barrier, len(peers))

    nxt = (ctx + 1) % (QUAD * RING)
    send(proj.at[pl.ds(1, 2), pl.ds(length - RIM, RIM), :], rim, TO_RIM, rim_r.at[0], at(nxt, tp))

    def qrim_copy(s):
        return rcopy(
            proj.at[0, pl.ds(length - RIM, RIM), pl.ds(s * piece, piece)],
            qext.at[pl.ds(0, RIM), :],
            sends.at[TO_QRIM], qrim_r.at[0], at(zu * QUAD + s, tp),
        )

    @pl.when(r == QUAD - 1)
    def _():
        for s in range(QUAD):
            qrim_copy(s).start()

    parts = (pl.ds(rows_step, length - rows_step), pl.ds(0, rows_step))

    def own_part_rows(rr, part):
        low, size = (rows_step, length - rows_step) if part == 0 else (0, rows_step)
        return pl.ds(pl.multiple_of(kept + rr * length + low, 16), size)

    def halo_part_rows(rr, part):
        low, size = (rows_step, length - rows_step) if part == 0 else (0, rows_step)
        return pl.ds(pl.multiple_of(rr * length + low, 16), size)

    def mix_send(s, part):
        send(
            mixsend.at[s, parts[part], :], seq.at[own_part_rows(r, part), :],
            TO_MIX, mix_r.at[2 * s + part], at(z * QUAD + flip(s), tp),
        )

    def halo_send(s, part):
        rr = flip(s)
        send(
            seq.at[own_part_rows(rr, part), :], seq.at[halo_part_rows(rr, part), :],
            TO_HALO, halo_r.at[rr], up,
        )

    def mix_pass(s, part):
        landed(seq.at[own_part_rows(flip(s), part), :], mix_r.at[2 * s + part])
        halo_send(s, part)

    @pl.when(soon)
    def _():
        for j in range(CHUNKS):
            wx_copy(j).start()

    for s in (2, 3):
        mix_send(s, 0)
    piece_loads[2].wait()
    mix_body(1)
    mix_send(1, 0)
    piece_loads[3].wait()
    mix_body(0)
    halo_send(0, 0)

    loads[1].wait()
    tile = half
    ii = lax.broadcasted_iota(jnp.int32, (tile, tile), 0)
    jj = lax.broadcasted_iota(jnp.int32, (tile, tile), 1)
    anti = jnp.where(ii + jj == tile - 1, 1.0, 0.0).astype(bf16)
    ntile = kept // tile
    wide = filt[...].astype(f32)
    stacked = jnp.concatenate([wide[:, k * tile : (k + 1) * tile] for k in range(ntile)], axis=0)
    turned = jnp.dot(stacked.astype(bf16), anti, preferred_element_type=f32)
    rows8 = filt.shape[0]
    for k in range(ntile):
        flipped[:, (ntile - 1 - k) * tile : (ntile - k) * tile] = turned[k * rows8 : (k + 1) * rows8]
    for g in range(groups_here):
        row = flipped[pl.ds(r * groups_here + g, 1), :]
        base = jnp.concatenate([jnp.zeros((1, half), f32), row, jnp.zeros((1, length), f32)], axis=1)
        base = jnp.broadcast_to(base, (16, base.shape[1]))
        base = pltpu.roll(base, 1, 1, stride=1, stride_axis=0)

        def band(k, carry):
            rolled = pltpu.roll(base, 16 * k, 1).astype(bf16)
            start = pl.multiple_of(16 * k, 16)
            strip[g, pl.ds(start, 16), :] = rolled[:, half:]
            strip[g, pl.ds(half + start, 16), :] = rolled[:, : kept + length]
            return carry

        lax.fori_loop(0, half // 16, band, 0)

    landed(rim, rim_r.at[0])
    for s in (2, 3, 1):
        mix_head(s)
        mix_send(s, 1)
    mix_head(0)
    halo_send(0, 1)
    wx_start(0)
    fixed_start(False)

    mix_pass(1, 0)
    mix_pass(1, 1)
    mix_pass(2, 0)
    mix_pass(3, 0)
    @pl.when(soon_here)
    def _():
        for j in EARLY:
            landed(wslot(z, j), wx_r.at[j])
            z_copy(j, wslot(z, j), False).start()

    for s in (2, 3, 1):
        lanes = pl.ds(pl.multiple_of(flip(s) * piece, piece), piece)
        send(proj.at[0, :, lanes], qext.at[qrows(r), :], TO_MIX, q_r.at[0], at(z * QUAD + flip(s), tp))
    for j in range(1, CHUNKS):
        wx_start(j)
    for s in (2, 3):
        mix_pass(s, 1)


    loads[2].wait()
    gains = gain[:, mine]
    def window_dot(b, g, first_block, last_block):
        lanes = slice(g * group_width, (g + 1) * group_width)
        rows = slice((b + first_block) * length, (b + last_block) * length)
        return jnp.dot(
            strip[g, :, first_block * length : last_block * length], seq[rows, lanes], preferred_element_type=f32
        )

    for b in range(QUAD - 1, -1, -1):
        for g in range(groups_here):
            lanes = slice(g * group_width, (g + 1) * group_width)
            skip = gains[:, lanes] * seq[kept + b * length : kept + (b + 1) * length, lanes].astype(f32)
            tsum[b * length : (b + 1) * length, lanes] = skip + window_dot(b, g, QUAD - b, QUAD + 1)
    fixed_start(True)
    wz_down(0)
    wz_up(0)
    for b in range(QUAD - 1, -1, -1):
        landed(seq.at[pl.ds(b * length, length), :], halo_r.at[b])
        for g in range(groups_here):
            lanes = slice(g * group_width, (g + 1) * group_width)
            tsum[b * length : (b + 1) * length, lanes] += window_dot(b, g, 0, QUAD - b)

    landed(qext.at[pl.ds(0, RIM), :], qrim_r.at[0])
    landed(qext.at[pl.ds(RIM, QUAD * length), :], q_r.at[0])
    qtap = [taps[0, pl.ds(j, 1), mine] for j in range(ktaps)]

    def aslot(yy, cc, b):
        return abuf.at[2 * yy + cc, pl.ds(b * length, length), :]

    def slots(count):
        return abuf.at[pl.ds(0, count)]

    def gate(b):
        def gate_rows(i, carry):
            start = pl.multiple_of(b * length + i * rows_step, 16)
            query = short_conv(qext[pl.ds(start, rows_step + RIM), :].astype(f32), qtap)
            abuf[2 * y + c, pl.ds(start, rows_step), :] = (query * tsum[pl.ds(start, rows_step), :]).astype(bf16)
            return carry

        lax.fori_loop(0, length // rows_step, gate_rows, 0)

    def a_send(b):
        gate(b)
        send(aslot(y, c, b), aslot(y, c, b), TO_A, a_r.at[b], right)
        send(aslot(y, c, b), aslot(y, c, b), TO_A, a_r.at[4 + b], left)
        send(aslot(y, c, b), aslot(y, c, b), TO_A, p_r.at[b], partner)

    def a_pass(b):
        landed(aslot(yd, c, b), a_r.at[b])
        if b >= 2:
            send(aslot(yd, c, b), aslot(yd, c, b), TO_A, a2_r.at[b], right)
        send(aslot(yd, c, b), aslot(yd, c, b), TO_A, p_r.at[b], partner)
        landed(aslot(yu, c, b), a_r.at[4 + b])
        if b < 2:
            send(aslot(yu, c, b), aslot(yu, c, b), TO_A, a2_r.at[b], left)
        send(aslot(yu, c, b), aslot(yu, c, b), TO_A, p_r.at[b], partner)

    def a_last(b):
        landed(aslot(y2, c, b), a2_r.at[b])
        send(aslot(y2, c, b), aslot(y2, c, b), TO_A, p_r.at[b], partner)

    same = c == hi
    apart = jnp.logical_not(same)
    delta = jnp.where(same, 0, 2)

    def c_copy(b, g):
        d = delta + (1 - lo if b >= 2 else lo)
        rsem = c_r.at[jnp.where(d == 0, CHUNKS, 0) + g]
        return rcopy(
            csend[g].at[b], crecv[g].at[d], sends.at[TO_C],
            rsem, at(z * QUAD + b, y * 2 + c),
        )

    def own_part(b):
        return jnp.logical_and(same, r == b)

    def c_step(b, first_group, count=1):
        lhs = jnp.concatenate(
            [abuf[k, b * length : (b + 1) * length, :] for k in range(2 * RING)], axis=1
        )
        groups = range(first_group, first_group + count)
        rhs = wbuf[first_group][...] if count == 1 else jnp.concatenate([wbuf[g][...] for g in groups], axis=1)
        part = jnp.dot(lhs, rhs, preferred_element_type=f32).astype(bf16)
        low = CUTS[first_group][0]
        for g in groups:
            here = part[:, (CUTS[g][0] - low) * unit : (sum(CUTS[g]) - low) * unit]
            csend[g][b] = here

            @pl.when(own_part(b))
            def _():
                crecv[g][0] = here

            @pl.when(jnp.logical_not(own_part(b)))
            def _():
                c_copy(b, g).start()

    def a_other(b):
        landed(slots(1), p_r.at[b])

    def finish(g):
        @pl.when(apart)
        def _():
            landed(crecv[g].at[0], c_r.at[CHUNKS + g])

        landed(crecv[g].at[pl.ds(1, 3)], c_r.at[g])
        total = crecv[g][0].astype(f32)
        for d in range(1, 4):
            total = total + crecv[g][d].astype(f32)
        out[:, cut(g)] = total.astype(bf16)

    first, second, third, fourth = ORDER

    def w_ready(j):
        landed(wslot(z2, j), w2_r.at[j])

    a_send(first)
    a_send(second)
    wz_down(1)
    wz_up(1)
    from_above(0)
    a_pass(first)
    a_send(third)
    from_above(1)
    wz_down(2)
    wz_up(2)
    a_pass(second)
    a_send(fourth)
    for j in (3, 4):
        wz_down(j)
        wz_up(j)
    a_last(first)
    from_below(0)
    w_ready(0)
    a_other(first)
    c_step(first, 0)
    a_pass(third)
    a_last(second)
    a_pass(fourth)
    from_below(2)
    a_other(second)
    c_step(second, 0)
    from_below(1)
    w_ready(1)
    c_step(first, 1)
    c_step(second, 1)
    a_last(third)
    a_last(fourth)
    from_below(3)
    from_below(4)
    a_other(third)
    c_step(third, 0, 2)
    a_other(fourth)
    c_step(fourth, 0, 2)
    for j in range(2, CHUNKS):
        from_above(j)
        if j not in UPWARD:
            from_below(j)
        w_ready(j)
        for b in ORDER:
            c_step(b, j)
    for g in range(CHUNKS):
        finish(g)

    landed(rim, sends.at[TO_RIM])
    landed(seq.at[pl.ds(0, 6 * length), :], sends.at[TO_MIX])
    landed(seq.at[pl.ds(0, 4 * length), :], sends.at[TO_HALO])
    landed(slots(6), sends.at[TO_Z])
    landed(slots(7), sends.at[TO_A])

    @pl.when(moves)
    def _():
        landed(slots(2), sends.at[TO_X])

    @pl.when(r == QUAD - 1)
    def _():
        landed(seq.at[pl.ds(0, QUAD * RIM), :], sends.at[TO_QRIM])

    @pl.when(same)
    def _():
        landed(slots(3), sends.at[TO_C])

    @pl.when(apart)
    def _():
        landed(slots(4), sends.at[TO_C])


def local(projected, short_taps, range_filter, skip_gain, out_weight):
    streams, length, width = projected.shape
    piece = width // QUAD
    groups, kept = range_filter.shape
    groups_here = groups // QUAD
    depth, columns = out_weight.shape
    bf16, f32 = jnp.bfloat16, jnp.float32
    hbm = pl.BlockSpec(memory_space=pltpu.HBM)
    dma = pltpu.SemaphoreType.DMA
    nc = CHUNKS
    widths = [size * columns // 16 for _, size in CUTS]
    counts = (8, 1, 1, 1, 8, 4, nc, 2 * nc, nc, 8, 4, 4, 2 * nc)
    return pl.pallas_call(
        kernel,
        out_shape=jax.ShapeDtypeStruct((length, columns), bf16),
        in_specs=[hbm] * 5,
        out_specs=pl.BlockSpec(memory_space=pltpu.VMEM),
        scratch_shapes=[
            pltpu.VMEM(short_taps.shape, f32),
            pltpu.VMEM((groups, kept), bf16),
            pltpu.VMEM((1, width), f32),
            pltpu.VMEM((2, length, width), bf16),
            dma((7,)),
            pltpu.VMEM((2, RIM, width), bf16),
            pltpu.VMEM((RIM + QUAD * length, piece), bf16),
            pltpu.VMEM((QUAD * length, piece), f32),
            pltpu.VMEM((QUAD, length, piece), bf16),
            pltpu.VMEM((kept + QUAD * length, piece), bf16),
            pltpu.VMEM((groups, kept), f32),
            pltpu.VMEM((groups_here, length, kept + length), bf16),
            pltpu.VMEM((RING * 2, QUAD * length, piece), bf16),
            tuple(pltpu.VMEM((RING * depth, wide), bf16) for wide in widths),
            tuple(pltpu.VMEM((QUAD, length, wide), bf16) for wide in widths),
            tuple(pltpu.VMEM((4, length, wide), bf16) for wide in widths),
        ]
        + [dma((n,)) for n in counts],
        compiler_params=pltpu.CompilerParams(
            collective_id=0, has_side_effects=True, vmem_limit_bytes=50 * 1024 * 1024
        ),
    )(*[pltpu.with_memory_space_constraint(v, pltpu.HBM) for v in (projected, short_taps, range_filter, skip_gain[None, :], out_weight)])


def solution(mesh):
    placed = (P(None, "ctx", "tp"), P(None, None, "tp"), P("tp", None), P("tp"), P("ctx", "tp"))
    return jax.shard_map(
        local, mesh=mesh, in_specs=placed, out_specs=P("ctx", "tp"), check_vma=False
    )
```

```python
import functools

import jax
import jax.numpy as jnp
from jax import lax
from jax.experimental import pallas as pl
from jax.experimental.pallas import tpu as pltpu
from jax.sharding import PartitionSpec as P

MESH = pl.DeviceIdType.MESH
RIM = 16
CUTS = ((0, 4), (4, 4), (8, 4), (12, 2), (14, 2))
CHUNKS = len(CUTS)
TO_RIM, TO_QRIM, TO_MIX, TO_HALO, TO_X, TO_Z, TO_A, TO_C = range(8)
RING = 4
QUAD = 4
UPWARD = (2, 3, 4)
EARLY = (0, 1)
ORDER = (0, 2, 1, 3)


def short_conv(extended, tap_rows):
    acc = tap_rows[0] * extended[RIM:]
    for lag in range(1, len(tap_rows)):
        acc = acc + tap_rows[lag] * pltpu.roll(extended, lag, axis=0)[RIM:]
    return acc


def kernel(
    proj, taps_in, filt_in, gain_in, w, out,
    taps, filt, gain, streams, local_s, rim, qext, tsum, mixsend, seq, flipped, strip, abuf, wbuf, csend, crecv,
    sends, rim_r, q_r, qrim_r, mix_r, halo_r, wx_r, wz_r, w2_r, a_r, a2_r, p_r, c_r,
):
    length = proj.shape[1]
    piece = proj.shape[2] // QUAD
    ktaps = taps.shape[1]
    groups_here = strip.shape[0]
    group_width = piece // groups_here
    kept = filt.shape[1]
    shard = w.shape[0]
    unit = w.shape[1] // 16
    half = length // 2
    rows_step = length // 4
    f32, bf16 = jnp.float32, jnp.bfloat16

    ctx, tp = lax.axis_index("ctx"), lax.axis_index("tp")
    z, r = ctx // QUAD, ctx % QUAD
    lo, c = r // 2, r % 2
    y, hi = tp // 2, tp % 2
    zu, zd = (z + 1) % RING, (z + RING - 1) % RING
    yu, yd = (y + 1) % RING, (y + RING - 1) % RING
    z2, y2 = (z + 2) % RING, (y + 2) % RING

    def cut(j):
        return pl.ds(CUTS[j][0] * unit, CUTS[j][1] * unit)

    def flip(s):
        b1 = 1 - lo if s & 2 else lo
        b0 = 1 - c if s & 1 else c
        return 2 * b1 + b0

    def at(ctx_, tp_):
        return {"ctx": ctx_, "tp": tp_}

    up, down = at(zu * QUAD + r, tp), at(zd * QUAD + r, tp)
    right, left = at(ctx, yu * 2 + hi), at(ctx, yd * 2 + hi)
    partner = at(z * QUAD + flip(1), tp)

    def rcopy(src, dst, ssem, rsem, dev):
        return pltpu.make_async_remote_copy(
            src_ref=src, dst_ref=dst, send_sem=ssem, recv_sem=rsem, device_id=dev, device_id_type=MESH
        )

    def landed(dst, rsem):
        pltpu.make_async_copy(dst, dst, rsem).wait()

    def send(src, dst, kind, rsem, dev):
        rcopy(src, dst, sends.at[kind], rsem, dev).start()

    barrier = pltpu.get_barrier_semaphore()
    peers = [at(z * QUAD + flip(s), tp) for s in range(1, QUAD)]
    peers += [at(z * QUAD + s, y * 2 + 1 - hi) for s in range(QUAD)]
    peers += [at(zz * QUAD + s, tp) for zz in (zu, zd) for s in range(QUAD)]
    peers += [right, left]
    for dev in peers:
        pl.semaphore_signal(barrier, inc=1, device_id=dev, device_id_type=MESH)
    mine = pl.ds(pl.multiple_of(r * piece, piece), piece)

    def qrows(rr):
        return pl.ds(pl.multiple_of(RIM + rr * length, 16), length)

    loads = [
        pltpu.make_async_copy(src, dst, q_r.at[0] if k == 3 else local_s.at[k])
        for k, (src, dst) in enumerate((
            (taps_in, taps), (filt_in, filt), (gain_in, gain),
            (proj.at[0, :, mine], qext.at[qrows(r), :]),
        ))
    ]
    lanes_of = [pl.ds(pl.multiple_of(flip(s) * piece, piece), piece) for s in (2, 3, 1, 0)]
    piece_loads = [
        pltpu.make_async_copy(proj.at[pl.ds(1, 2), :, lanes], streams.at[:, :, lanes], local_s.at[3 + k])
        for k, lanes in enumerate(lanes_of)
    ]
    for load in loads[:1] + piece_loads + loads[1:]:
        load.start()

    fixed = jnp.logical_and(c == hi, hi == lo)
    moves = jnp.logical_not(fixed)
    wdst = at(z * QUAD + 2 * c + hi, y * 2 + lo)

    def wslot(zz, j):
        return wbuf[j].at[pl.ds(pl.multiple_of(zz * shard, shard), shard), :]

    def wx_copy(j):
        return rcopy(w.at[:, cut(j)], wslot(z, j), sends.at[TO_X], wx_r.at[j], wdst)

    soon = jnp.logical_and(lo != hi, c == hi)
    soon_here = jnp.logical_and(lo != hi, c == lo)

    def wx_start(j):
        @pl.when(jnp.logical_and(moves, jnp.logical_not(soon)))
        def _():
            wx_copy(j).start()

    def z_copy(j, src, upward):
        if upward:
            return rcopy(src, wslot(z, j), sends.at[TO_Z], wz_r.at[j], up)
        return rcopy(src, wslot(z, j), sends.at[TO_Z], wz_r.at[CHUNKS + j], down)

    def fixed_start(upward):
        @pl.when(fixed)
        def _():
            for j in range(CHUNKS):
                if not upward:
                    pltpu.make_async_copy(w.at[:, cut(j)], wslot(z, j), wx_r.at[j]).start()
                z_copy(j, w.at[:, cut(j)], upward).start()

    def wz_down(j):
        late = jnp.logical_not(soon_here) if j in EARLY else True

        @pl.when(late)
        def _():
            landed(wslot(z, j), wx_r.at[j])

        @pl.when(jnp.logical_and(moves, late))
        def _():
            z_copy(j, wslot(z, j), False).start()

    def wz_up(j):
        @pl.when(moves)
        def _():
            z_copy(j, wslot(z, j), True).start()

    def from_below(j):
        landed(wslot(zd, j), wz_r.at[j])
        if j in UPWARD:
            send(wslot(zd, j), wslot(zd, j), TO_Z, w2_r.at[j], up)

    def from_above(j):
        landed(wslot(zu, j), wz_r.at[CHUNKS + j])
        if j not in UPWARD:
            send(wslot(zu, j), wslot(zu, j), TO_Z, w2_r.at[j], down)

    def own_rows(rr):
        return pl.ds(pl.multiple_of(kept + rr * length, length), length)

    def halo_rows(rr):
        return pl.ds(pl.multiple_of(rr * length, length), length)

    def mix_dst(s):
        return mixsend.at[s] if s else seq.at[own_rows(r), :]

    def piece_taps(s):
        lanes = pl.ds(pl.multiple_of(flip(s) * piece, piece), piece)
        return lanes, [[taps[m, pl.ds(j, 1), lanes] for j in range(ktaps)] for m in (1, 2)]

    def mix_body(s):
        lanes, (ktap, vtap) = piece_taps(s)
        dst = mix_dst(s)

        def rows(i, carry):
            start = pl.multiple_of(i * rows_step - RIM, 16)
            key = streams[0, pl.ds(start, rows_step + RIM), lanes].astype(f32)
            value = streams[1, pl.ds(start, rows_step + RIM), lanes].astype(f32)
            product = short_conv(key, ktap) * short_conv(value, vtap)
            dst[pl.ds(pl.multiple_of(i * rows_step, 16), rows_step), :] = product.astype(bf16)
            return carry

        lax.fori_loop(1, length // rows_step, rows, 0)

    def mix_head(s):
        lanes, (ktap, vtap) = piece_taps(s)
        key = jnp.concatenate([rim[0, :, lanes], streams[0, pl.ds(0, rows_step), lanes]], axis=0).astype(f32)
        value = jnp.concatenate([rim[1, :, lanes], streams[1, pl.ds(0, rows_step), lanes]], axis=0).astype(f32)
        product = short_conv(key, ktap) * short_conv(value, vtap)
        mix_dst(s)[pl.ds(0, rows_step), :] = product.astype(bf16)

    loads[0].wait()
    for k, s in enumerate((2, 3)):
        piece_loads[k].wait()
        mix_body(s)

    pl.semaphore_wait(barrier, len(peers))

    nxt = (ctx + 1) % (QUAD * RING)
    send(proj.at[pl.ds(1, 2), pl.ds(length - RIM, RIM), :], rim, TO_RIM, rim_r.at[0], at(nxt, tp))

    def qrim_copy(s):
        return rcopy(
            proj.at[0, pl.ds(length - RIM, RIM), pl.ds(s * piece, piece)],
            qext.at[pl.ds(0, RIM), :],
            sends.at[TO_QRIM], qrim_r.at[0], at(zu * QUAD + s, tp),
        )

    @pl.when(r == QUAD - 1)
    def _():
        for s in range(QUAD):
            qrim_copy(s).start()

    parts = (pl.ds(rows_step, length - rows_step), pl.ds(0, rows_step))

    def own_part_rows(rr, part):
        low, size = (rows_step, length - rows_step) if part == 0 else (0, rows_step)
        return pl.ds(pl.multiple_of(kept + rr * length + low, 16), size)

    def halo_part_rows(rr, part):
        low, size = (rows_step, length - rows_step) if part == 0 else (0, rows_step)
        return pl.ds(pl.multiple_of(rr * length + low, 16), size)

    def mix_send(s, part):
        send(
            mixsend.at[s, parts[part], :], seq.at[own_part_rows(r, part), :],
            TO_MIX, mix_r.at[2 * s + part], at(z * QUAD + flip(s), tp),
        )

    def halo_send(s, part):
        rr = flip(s)
        send(
            seq.at[own_part_rows(rr, part), :], seq.at[halo_part_rows(rr, part), :],
            TO_HALO, halo_r.at[rr], up,
        )

    def mix_pass(s, part):
        landed(seq.at[own_part_rows(flip(s), part), :], mix_r.at[2 * s + part])
        halo_send(s, part)

    @pl.when(soon)
    def _():
        for j in range(CHUNKS):
            wx_copy(j).start()

    for s in (2, 3):
        mix_send(s, 0)
    piece_loads[2].wait()
    mix_body(1)
    mix_send(1, 0)
    piece_loads[3].wait()
    mix_body(0)
    halo_send(0, 0)

    loads[1].wait()
    tile = half
    ii = lax.broadcasted_iota(jnp.int32, (tile, tile), 0)
    jj = lax.broadcasted_iota(jnp.int32, (tile, tile), 1)
    anti = jnp.where(ii + jj == tile - 1, 1.0, 0.0).astype(bf16)
    ntile = kept // tile
    wide = filt[...].astype(f32)
    stacked = jnp.concatenate([wide[:, k * tile : (k + 1) * tile] for k in range(ntile)], axis=0)
    turned = jnp.dot(stacked.astype(bf16), anti, preferred_element_type=f32)
    rows8 = filt.shape[0]
    for k in range(ntile):
        flipped[:, (ntile - 1 - k) * tile : (ntile - k) * tile] = turned[k * rows8 : (k + 1) * rows8]
    for g in range(groups_here):
        row = flipped[pl.ds(r * groups_here + g, 1), :]
        base = jnp.concatenate([jnp.zeros((1, half), f32), row, jnp.zeros((1, length), f32)], axis=1)
        base = jnp.broadcast_to(base, (16, base.shape[1]))
        base = pltpu.roll(base, 1, 1, stride=1, stride_axis=0)

        def band(k, carry):
            rolled = pltpu.roll(base, 16 * k, 1).astype(bf16)
            start = pl.multiple_of(16 * k, 16)
            strip[g, pl.ds(start, 16), :] = rolled[:, half:]
            strip[g, pl.ds(half + start, 16), :] = rolled[:, : kept + length]
            return carry

        lax.fori_loop(0, half // 16, band, 0)

    landed(rim, rim_r.at[0])
    for s in (2, 3, 1):
        mix_head(s)
        mix_send(s, 1)
    mix_head(0)
    halo_send(0, 1)
    wx_start(0)
    fixed_start(False)

    mix_pass(1, 0)
    mix_pass(1, 1)
    mix_pass(2, 0)
    mix_pass(3, 0)
    @pl.when(soon_here)
    def _():
        for j in EARLY:
            landed(wslot(z, j), wx_r.at[j])
            z_copy(j, wslot(z, j), False).start()

    for s in (2, 3, 1):
        lanes = pl.ds(pl.multiple_of(flip(s) * piece, piece), piece)
        send(proj.at[0, :, lanes], qext.at[qrows(r), :], TO_MIX, q_r.at[0], at(z * QUAD + flip(s), tp))
    for j in range(1, CHUNKS):
        wx_start(j)
    for s in (2, 3):
        mix_pass(s, 1)


    loads[2].wait()
    gains = gain[:, mine]
    def window_dot(b, g, first_block, last_block):
        lanes = slice(g * group_width, (g + 1) * group_width)
        rows = slice((b + first_block) * length, (b + last_block) * length)
        return jnp.dot(
            strip[g, :, first_block * length : last_block * length], seq[rows, lanes], preferred_element_type=f32
        )

    for b in range(QUAD - 1, -1, -1):
        for g in range(groups_here):
            lanes = slice(g * group_width, (g + 1) * group_width)
            skip = gains[:, lanes] * seq[kept + b * length : kept + (b + 1) * length, lanes].astype(f32)
            tsum[b * length : (b + 1) * length, lanes] = skip + window_dot(b, g, QUAD - b, QUAD + 1)
    fixed_start(True)
    wz_down(0)
    wz_up(0)
    for b in range(QUAD - 1, -1, -1):
        landed(seq.at[pl.ds(b * length, length), :], halo_r.at[b])
        for g in range(groups_here):
            lanes = slice(g * group_width, (g + 1) * group_width)
            tsum[b * length : (b + 1) * length, lanes] += window_dot(b, g, 0, QUAD - b)

    landed(qext.at[pl.ds(0, RIM), :], qrim_r.at[0])
    landed(qext.at[pl.ds(RIM, QUAD * length), :], q_r.at[0])
    qtap = [taps[0, pl.ds(j, 1), mine] for j in range(ktaps)]

    def aslot(yy, cc, b):
        return abuf.at[2 * yy + cc, pl.ds(b * length, length), :]

    def slots(count):
        return abuf.at[pl.ds(0, count)]

    def gate(b):
        def gate_rows(i, carry):
            start = pl.multiple_of(b * length + i * rows_step, 16)
            query = short_conv(qext[pl.ds(start, rows_step + RIM), :].astype(f32), qtap)
            abuf[2 * y + c, pl.ds(start, rows_step), :] = (query * tsum[pl.ds(start, rows_step), :]).astype(bf16)
            return carry

        lax.fori_loop(0, length // rows_step, gate_rows, 0)

    def a_send(b):
        gate(b)
        send(aslot(y, c, b), aslot(y, c, b), TO_A, a_r.at[b], right)
        send(aslot(y, c, b), aslot(y, c, b), TO_A, a_r.at[4 + b], left)
        send(aslot(y, c, b), aslot(y, c, b), TO_A, p_r.at[b], partner)

    def a_pass(b):
        landed(aslot(yd, c, b), a_r.at[b])
        if b >= 2:
            send(aslot(yd, c, b), aslot(yd, c, b), TO_A, a2_r.at[b], right)
        send(aslot(yd, c, b), aslot(yd, c, b), TO_A, p_r.at[b], partner)
        landed(aslot(yu, c, b), a_r.at[4 + b])
        if b < 2:
            send(aslot(yu, c, b), aslot(yu, c, b), TO_A, a2_r.at[b], left)
        send(aslot(yu, c, b), aslot(yu, c, b), TO_A, p_r.at[b], partner)

    def a_last(b):
        landed(aslot(y2, c, b), a2_r.at[b])
        send(aslot(y2, c, b), aslot(y2, c, b), TO_A, p_r.at[b], partner)

    same = c == hi
    apart = jnp.logical_not(same)
    delta = jnp.where(same, 0, 2)

    def c_copy(b, g):
        d = delta + (1 - lo if b >= 2 else lo)
        rsem = c_r.at[jnp.where(d == 0, CHUNKS, 0) + g]
        return rcopy(
            csend[g].at[b], crecv[g].at[d], sends.at[TO_C],
            rsem, at(z * QUAD + b, y * 2 + c),
        )

    def own_part(b):
        return jnp.logical_and(same, r == b)

    def c_step(b, first_group, count=1):
        lhs = jnp.concatenate(
            [abuf[k, b * length : (b + 1) * length, :] for k in range(2 * RING)], axis=1
        )
        groups = range(first_group, first_group + count)
        rhs = wbuf[first_group][...] if count == 1 else jnp.concatenate([wbuf[g][...] for g in groups], axis=1)
        part = jnp.dot(lhs, rhs, preferred_element_type=f32).astype(bf16)
        low = CUTS[first_group][0]
        for g in groups:
            here = part[:, (CUTS[g][0] - low) * unit : (sum(CUTS[g]) - low) * unit]
            csend[g][b] = here

            @pl.when(own_part(b))
            def _():
                crecv[g][0] = here

            @pl.when(jnp.logical_not(own_part(b)))
            def _():
                c_copy(b, g).start()

    def a_other(b):
        landed(slots(1), p_r.at[b])

    def finish(g):
        @pl.when(apart)
        def _():
            landed(crecv[g].at[0], c_r.at[CHUNKS + g])

        landed(crecv[g].at[pl.ds(1, 3)], c_r.at[g])
        total = crecv[g][0].astype(f32)
        for d in range(1, 4):
            total = total + crecv[g][d].astype(f32)
        out[:, cut(g)] = total.astype(bf16)

    first, second, third, fourth = ORDER

    def w_ready(j):
        landed(wslot(z2, j), w2_r.at[j])

    a_send(first)
    a_send(second)
    wz_down(1)
    wz_up(1)
    from_above(0)
    a_pass(first)
    a_send(third)
    from_above(1)
    wz_down(2)
    wz_up(2)
    a_pass(second)
    a_send(fourth)
    for j in (3, 4):
        wz_down(j)
        wz_up(j)
    a_last(first)
    from_below(0)
    w_ready(0)
    a_other(first)
    c_step(first, 0)
    a_pass(third)
    a_last(second)
    a_pass(fourth)
    from_below(2)
    a_other(second)
    c_step(second, 0)
    from_below(1)
    w_ready(1)
    c_step(first, 1)
    c_step(second, 1)
    a_last(third)
    a_last(fourth)
    from_below(3)
    from_below(4)
    a_other(third)
    c_step(third, 0, 2)
    a_other(fourth)
    c_step(fourth, 0, 2)
    for j in range(2, CHUNKS):
        from_above(j)
        if j not in UPWARD:
            from_below(j)
        w_ready(j)
        for b in ORDER:
            c_step(b, j)
    for g in range(CHUNKS):
        finish(g)

    landed(rim, sends.at[TO_RIM])
    landed(seq.at[pl.ds(0, 6 * length), :], sends.at[TO_MIX])
    landed(seq.at[pl.ds(0, 4 * length), :], sends.at[TO_HALO])
    landed(slots(6), sends.at[TO_Z])
    landed(slots(7), sends.at[TO_A])

    @pl.when(moves)
    def _():
        landed(slots(2), sends.at[TO_X])

    @pl.when(r == QUAD - 1)
    def _():
        landed(seq.at[pl.ds(0, QUAD * RIM), :], sends.at[TO_QRIM])

    @pl.when(same)
    def _():
        landed(slots(3), sends.at[TO_C])

    @pl.when(apart)
    def _():
        landed(slots(4), sends.at[TO_C])


def local(projected, short_taps, range_filter, skip_gain, out_weight):
    streams, length, width = projected.shape
    piece = width // QUAD
    groups, kept = range_filter.shape
    groups_here = groups // QUAD
    depth, columns = out_weight.shape
    bf16, f32 = jnp.bfloat16, jnp.float32
    hbm = pl.BlockSpec(memory_space=pltpu.HBM)
    dma = pltpu.SemaphoreType.DMA
    nc = CHUNKS
    widths = [size * columns // 16 for _, size in CUTS]
    counts = (8, 1, 1, 1, 8, 4, nc, 2 * nc, nc, 8, 4, 4, 2 * nc)
    return pl.pallas_call(
        kernel,
        out_shape=jax.ShapeDtypeStruct((length, columns), bf16),
        in_specs=[hbm] * 5,
        out_specs=pl.BlockSpec(memory_space=pltpu.VMEM),
        scratch_shapes=[
            pltpu.VMEM(short_taps.shape, f32),
            pltpu.VMEM((groups, kept), bf16),
            pltpu.VMEM((1, width), f32),
            pltpu.VMEM((2, length, width), bf16),
            dma((7,)),
            pltpu.VMEM((2, RIM, width), bf16),
            pltpu.VMEM((RIM + QUAD * length, piece), bf16),
            pltpu.VMEM((QUAD * length, piece), f32),
            pltpu.VMEM((QUAD, length, piece), bf16),
            pltpu.VMEM((kept + QUAD * length, piece), bf16),
            pltpu.VMEM((groups, kept), f32),
            pltpu.VMEM((groups_here, length, kept + length), bf16),
            pltpu.VMEM((RING * 2, QUAD * length, piece), bf16),
            tuple(pltpu.VMEM((RING * depth, wide), bf16) for wide in widths),
            tuple(pltpu.VMEM((QUAD, length, wide), bf16) for wide in widths),
            tuple(pltpu.VMEM((4, length, wide), bf16) for wide in widths),
        ]
        + [dma((n,)) for n in counts],
        compiler_params=pltpu.CompilerParams(
            collective_id=0, has_side_effects=True, vmem_limit_bytes=50 * 1024 * 1024
        ),
    )(*[pltpu.with_memory_space_constraint(v, pltpu.HBM) for v in (projected, short_taps, range_filter, skip_gain[None, :], out_weight)])


def solution(mesh):
    placed = (P(None, "ctx", "tp"), P(None, None, "tp"), P("tp", None), P("tp"), P("ctx", "tp"))
    return jax.shard_map(
        local, mesh=mesh, in_specs=placed, out_specs=P("ctx", "tp"), check_vma=False
    )
```
